32 devices in a mesh: grp: 2 (over y), mem: 8 (over z, x), slab: 2 (over core).
Axes of the slice: x: 2, y: 2, z: 4, core: 2. Of those that a mesh axis runs over, the one named last changes fastest.
Arguments:
- parameter_field: float32 [32, 32, 32, 256], P(('grp', 'mem'), 'slab'), parts along dimension 0, may hold values from -5 to 5
- initial_tracer: float32 [64, 32, 256], P(('grp', 'slab')), parts along dimension 0, may hold values from -1 to 1
- observed: float32 [8192], P(('grp', 'slab')), parts along dimension 0, may hold values from -3 to 3
- observation_variance: float32 [8192], P(('grp', 'slab')), parts along dimension 0, may hold values from 0.25 to 2.5
- observation_index: int32 [8192], P(('grp', 'slab')), parts along dimension 0, may hold values from 0 to 262143, as said below
- noise: float32 [32, 16], P('grp'), parts along dimension 0, may hold values from -6 to 6
Outputs:
- new_field: float32 [32, 32, 32, 256], P(('grp', 'mem'), 'slab'), parts along dimension 0
- predicted: float32 [32, 4096], P(('grp', 'mem'), 'slab'), parts along dimension 0
- mixing: float32 [32, 16], P(('grp', 'mem')), parts along dimension 0
The draws below stay inside these ranges and needn't reach their ends.
There are 2 independent parts, one for each index of `grp`. The reference program is written for one: setup_inputs(seed, part) draws one part's arguments, and reference() takes and returns one part's arrays. A program takes and returns all parts, laid end to end along the dimension named above; each array names one. Nothing has to cross between parts.
Inputs may be any that keep to these rules, and one draw needn't show every extreme that they name: `observation_index`: observation i names a flattened cell whose x lies in x-slab i // 2048, that is from (i // 2048) * 16 to (i // 2048) * 16 + 15; cells may repeat.
All inputs are finite; a program needn't handle non-finite values.
Results may differ from the reference program's by a relative error of at most 0.00011.
Values sent between devices are 32-bit elements; how exact they have to be, the bound alone decides.
No kernel may reach another device: no remote copies, remote signals or barrier semaphores. Data moves between devices by JAX's collectives and lax.ppermute only.
A program may use at most 192 MiB of HBM per device.

```python
import math
import jax
import jax.numpy as jnp
from jax import lax

CX = 16
NZ = 32
NY = 256
STEPS = 3
OBS_SLAB = 2048
NX = 32
MEMBERS = 16
OBS = 4096


def draw_observation_index(key, part):
    key_x = jax.random.fold_in(key, 101)
    key_z = jax.random.fold_in(key, 202)
    key_y = jax.random.fold_in(key, 303)
    owner = jnp.arange(OBS, dtype=jnp.int32) // OBS_SLAB
    column_x = owner * CX + jax.random.randint(key_x, (OBS,), 0, CX, dtype=jnp.int32)
    column_z = jax.random.randint(key_z, (OBS,), 0, NZ, dtype=jnp.int32)
    column_y = jax.random.randint(key_y, (OBS,), 0, NY, dtype=jnp.int32)
    flat_cell = (column_x * NZ + column_z) * NY + column_y
    flat_cell = flat_cell.at[0].set(0).at[OBS - 1].set(NX * NZ * NY - 1)
    return flat_cell.astype(jnp.int32)


def steps_of(rng, shape, pieces, smallest, top_value):
    loudness, own = 1.0, jax.random.fold_in(rng, 6)
    for axis_at, blocks in pieces:
        draws = jnp.exp(jax.random.uniform(jax.random.fold_in(own, axis_at), (blocks,), jnp.float32, smallest / len(pieces), top_value / len(pieces)))
        loudness = loudness * jnp.repeat(draws, shape[axis_at] // blocks).reshape([-1 if axis == axis_at else 1 for axis in range(len(shape))])
    return loudness


def bell_draw(own_key, dims, spread, bound, split=(), kind=jnp.bfloat16):
    result = spread * jax.random.normal(own_key, dims, jnp.float32)
    if split:
        result = result * steps_of(own_key, dims, split, -0.22, 0.18)
    return jnp.clip(result, -bound, bound).astype(kind)


def setup_inputs(seed: int = 0, part: int = 0) -> dict:
    keys = jax.random.split(jax.random.key(seed), 7)
    part_splits = jax.random.split(jax.random.fold_in(keys[6], part), 7)
    parameter_field = bell_draw(part_splits[0], (MEMBERS, NX, NZ, NY), 1.0, 5.0, ((0, 8), (1, 2)), jnp.float32)
    initial_tracer = jnp.clip(jax.random.uniform(part_splits[1], (NX, NZ, NY), jnp.float32, -1.0, 1.0) * steps_of(part_splits[1], (NX, NZ, NY), ((0, 2),), -0.4, 0.0), -1.0, 1.0)
    observed = bell_draw(part_splits[2], (OBS,), 0.5, 3.0, ((0, 2),), jnp.float32)
    observation_variance = jnp.clip(jnp.exp(math.log(2.5) - 2.3025851 * jax.random.uniform(part_splits[3], (OBS,), jnp.float32) ** steps_of(part_splits[3], (OBS,), ((0, 2),), -0.2, 0.2)), 0.25, 2.5)
    observation_index = draw_observation_index(jax.random.fold_in(jax.random.fold_in(keys[6], part), 71), part)
    noise = bell_draw(part_splits[5], (MEMBERS, MEMBERS), 1.0, 6.0, (), jnp.float32)
    return {"parameter_field": parameter_field, "initial_tracer": initial_tracer, "observed": observed, "observation_variance": observation_variance, "observation_index": observation_index, "noise": noise}


ADVECT_SPEED = 0.1
KAPPA_BASE = 0.07
KAPPA_SWING = 0.05
STEP_SCALE = 0.02
PRIOR_VARIANCE = 0.02
EPSILON = 1e-06

def advance(extended, diffusivity):
    center = extended[:, 1:-1]
    upper_level = jnp.concatenate([center[:, :, 1:], center[:, :, -1:]], axis=2)
    lower_level = jnp.concatenate([center[:, :, :1], center[:, :, :-1]], axis=2)
    laplace = extended[:, 2:] + extended[:, :-2] + upper_level + lower_level + jnp.roll(center, 1, axis=3) + jnp.roll(center, -1, axis=3) - 6.0 * center
    fluxes = 0.5 * ADVECT_SPEED * extended * extended
    wave_speed = ADVECT_SPEED * jnp.maximum(jnp.abs(extended[:, :-1]), jnp.abs(extended[:, 1:]))
    face_flux = 0.5 * (fluxes[:, :-1] + fluxes[:, 1:]) - 0.5 * wave_speed * (extended[:, 1:] - extended[:, :-1])
    return center + diffusivity * laplace - (face_flux[:, 1:] - face_flux[:, :-1])

def reference(parameter_field, initial_tracer, observed, observation_variance, observation_index, noise):

    def forward(member_field):
        diffusivity = (KAPPA_BASE + KAPPA_SWING * jnp.tanh(member_field))[None]
        tracer = initial_tracer[None]
        for step_number in range(STEPS):
            extended = jnp.concatenate([tracer[:, -1:], tracer, tracer[:, :1]], axis=1)
            tracer = advance(extended, diffusivity)
        return jnp.take(tracer[0].reshape(-1), observation_index, axis=0)
    predicted = lax.map(forward, parameter_field)
    member_mean = lax.optimization_barrier(jnp.mean(predicted, axis=0, keepdims=True))
    spread_obs = predicted - member_mean
    weighted = (predicted - observed[None]) / observation_variance[None]
    data_gram = jnp.dot(spread_obs, weighted.T, precision=lax.Precision.HIGHEST, preferred_element_type=jnp.float32) / MEMBERS
    flattened = parameter_field.reshape(MEMBERS, -1)
    field_mean = lax.optimization_barrier(jnp.mean(flattened, axis=0, keepdims=True))
    deviation = flattened - field_mean
    prior_gram = jnp.dot(deviation, flattened.T, precision=lax.Precision.HIGHEST, preferred_element_type=jnp.float32) / (MEMBERS * PRIOR_VARIANCE * NX * NZ * NY)
    step_size = STEP_SCALE / jnp.sqrt(jnp.mean(data_gram * data_gram) + EPSILON)
    mixing = -step_size * (data_gram + prior_gram) + jnp.sqrt(2.0 * step_size / MEMBERS) * noise
    updated = flattened + jnp.dot(mixing.T, deviation, precision=lax.Precision.HIGHEST, preferred_element_type=jnp.float32)
    new_field = updated.reshape(MEMBERS, NX, NZ, NY)
    return (new_field, predicted, mixing)
```

```python
import functools

import jax
import jax.numpy as jnp
from jax import lax
from jax.experimental import pallas as pl
from jax.experimental.pallas import tpu as pltpu
from jax.sharding import PartitionSpec as P

STEPS = 3

ADVECT_SPEED = 0.1
KAPPA_BASE = 0.07
KAPPA_SWING = 0.05
STEP_SCALE = 0.02
PRIOR_VARIANCE = 0.02
EPSILON = 1e-06

LANES = 128
SUBLANES = 8


def ring(axis):
    count = lax.axis_size(axis)
    forward = [(i, (i + 1) % count) for i in range(count)]
    backward = [(target, source) for source, target in forward]
    return forward, backward


def face_flux(left, right):
    mean_flux = 0.5 * (0.5 * ADVECT_SPEED * left * left + 0.5 * ADVECT_SPEED * right * right)
    speed = ADVECT_SPEED * jnp.maximum(jnp.abs(left), jnp.abs(right))
    return mean_flux - 0.5 * speed * (right - left)


def laplacian(below, center, above, first_level, last_level):
    levels, columns = center.shape
    upper = jnp.where(last_level, center, pltpu.roll(center, levels - 1, 0))
    lower = jnp.where(first_level, center, pltpu.roll(center, 1, 0))
    return (
        above
        + below
        + upper
        + lower
        + pltpu.roll(center, 1, 1)
        + pltpu.roll(center, columns - 1, 1)
        - 6.0 * center
    )


def forward_kernel(
    index_ref, tracer_ref, param_ref, low_ref, high_ref, out_ref, ext, kappa, buf_a, buf_b, table
):
    members, width, levels, columns = param_ref.shape
    rim = STEPS - 1
    halves = columns // LANES
    pitch = table.shape[0] // (width * levels * halves)
    row = lax.broadcasted_iota(jnp.int32, (levels, columns), 0)
    first_level = row == 0
    last_level = row == levels - 1

    for i in range(STEPS):
        ext[i] = low_ref[i]
        ext[STEPS + width + i] = high_ref[i]

    @pl.loop(0, width)
    def _(i):
        ext[STEPS + i] = tracer_ref[i]
        for m in range(members):
            kappa[m, rim + i] = KAPPA_BASE + KAPPA_SWING * jnp.tanh(param_ref[m, i])

    for m in range(members):
        for i in range(rim):
            at = STEPS + m * rim + i
            kappa[m, i] = KAPPA_BASE + KAPPA_SWING * jnp.tanh(low_ref[at])
            kappa[m, rim + width + i] = KAPPA_BASE + KAPPA_SWING * jnp.tanh(high_ref[at])

    def step_first(i, carry):
        below, center, flux_low = carry
        above = ext[i + 2]
        flux_high = face_flux(center, above)
        lap = laplacian(below, center, above, first_level, last_level)
        base = center - (flux_high - flux_low)
        for m in range(members):
            buf_a[m, i] = base + kappa[m, i] * lap
        return center, above, flux_high

    lax.fori_loop(
        0, width + 2 * rim, step_first, (ext[0], ext[1], face_flux(ext[0], ext[1]))
    )

    for number in range(1, STEPS):
        source, target = (buf_a, buf_b) if number % 2 else (buf_b, buf_a)
        margin = STEPS - 1 - number
        last = number == STEPS - 1
        for m in range(members):

            def step_next(i, carry):
                below, center, flux_low = carry
                above = source[m, i + 2]
                flux_high = face_flux(center, above)
                lap = laplacian(below, center, above, first_level, last_level)
                new = center - (flux_high - flux_low) + kappa[m, i + number] * lap
                if last:
                    for h in range(halves):
                        at = i * (levels * halves * pitch) + h * pitch + m
                        table[pl.ds(at, levels, stride=halves * pitch), :] = new[
                            :, h * LANES : (h + 1) * LANES
                        ]
                else:
                    target[m, i] = new
                return center, above, flux_high

            start = (source[m, 0], source[m, 1], face_flux(source[m, 0], source[m, 1]))
            lax.fori_loop(0, width + 2 * margin, step_next, start)

    first_cell = lax.axis_index("slab") * (width * levels * columns)
    lane = lax.broadcasted_iota(jnp.int32, (SUBLANES, LANES), 1)

    @pl.loop(0, out_ref.shape[1] // LANES)
    def _(group):
        first = group * LANES
        picked = jnp.zeros((SUBLANES, LANES), jnp.float32)
        for o in range(LANES):
            cell = index_ref[first + o] - first_cell
            at = pl.multiple_of(lax.shift_right_logical(cell, 7) * pitch, pitch)
            rows = table[pl.ds(at, SUBLANES), :]
            turn = (o - cell) & (LANES - 1)
            picked = jnp.where(lane == o, pltpu.roll(rows, turn, 1), picked)
        out_ref[:, pl.ds(pl.multiple_of(first, LANES), LANES)] = picked[:members]


def forward_observe(index, tracer, param, low, high):
    members, width, levels, columns = param.shape
    rim = STEPS - 1
    pitch = SUBLANES
    rows = width * levels * (columns // LANES) * pitch
    vmem = pl.BlockSpec(memory_space=pltpu.VMEM)
    return pl.pallas_call(
        forward_kernel,
        out_shape=jax.ShapeDtypeStruct((members, index.shape[0]), jnp.float32),
        in_specs=[pl.BlockSpec(memory_space=pltpu.SMEM), vmem, vmem, vmem, vmem],
        out_specs=vmem,
        scratch_shapes=[
            pltpu.VMEM((width + 2 * STEPS, levels, columns), jnp.float32),
            pltpu.VMEM((members, width + 2 * rim, levels, columns), jnp.float32),
            pltpu.VMEM((members, width + 2 * rim, levels, columns), jnp.float32),
            pltpu.VMEM((members, width + 2 * rim, levels, columns), jnp.float32),
            pltpu.VMEM((rows, LANES), jnp.float32),
        ],
        cost_estimate=pl.CostEstimate(
            flops=100 * param.size, bytes_accessed=16 * param.size, transcendentals=param.size
        ),
        name="forward_observe",
    )(index, tracer, param, low, high)


def dot32(spec, a, b):
    return jnp.einsum(
        spec, a, b, precision=lax.Precision.HIGHEST, preferred_element_type=jnp.float32
    )


def per_device(
    parameter_field, initial_tracer, observed, observation_variance, observation_index, noise
):
    members_here, slab_width, levels, columns = parameter_field.shape
    ensemble = noise.shape[0]
    owners = lax.axis_size("mem")
    slabs = lax.axis_size("slab")
    cell_rows = slab_width * levels
    rows = cell_rows // owners
    total_cells = cell_rows * columns * slabs
    rim = STEPS - 1

    forward, backward = ring("slab")
    side = (members_here * rim, levels, columns)
    to_high = jnp.concatenate(
        [initial_tracer[-STEPS:], parameter_field[:, -rim:].reshape(side)], axis=0
    )
    to_low = jnp.concatenate(
        [initial_tracer[:STEPS], parameter_field[:, :rim].reshape(side)], axis=0
    )
    low = lax.ppermute(to_high, "slab", forward)
    high = lax.ppermute(to_low, "slab", backward)

    blocks = parameter_field.reshape(members_here, owners, rows, columns).transpose(1, 0, 2, 3)
    spread = lax.all_to_all(blocks, "mem", split_axis=0, concat_axis=0, tiled=True)

    predicted = forward_observe(
        observation_index, initial_tracer, parameter_field, low, high
    )

    flat = spread.reshape(ensemble, rows * columns)
    deviation = flat - jnp.mean(flat, axis=0, keepdims=True)
    prior_part = dot32("kc,jc->kj", deviation, flat)

    seen = predicted.reshape(-1)
    load = jnp.concatenate([seen, prior_part.reshape(-1)]).reshape(-1, LANES)
    everyone = lax.all_to_all(
        jnp.broadcast_to(load[None], (owners,) + load.shape),
        "mem",
        split_axis=0,
        concat_axis=0,
        tiled=True,
    )
    cut = seen.size // LANES
    values = everyone[:, :cut].reshape(ensemble, -1)
    prior_part = jnp.sum(everyone[:, cut:], axis=0).reshape(ensemble, ensemble)

    spread_obs = values - jnp.mean(values, axis=0, keepdims=True)
    weighted = (values - observed[None]) / observation_variance[None]
    data_part = dot32("ko,jo->kj", spread_obs, weighted)

    both = jnp.stack([data_part, prior_part])
    both = lax.psum(both, "slab")
    data_gram = both[0] / ensemble
    prior_gram = both[1] / (ensemble * PRIOR_VARIANCE * total_cells)
    step_size = STEP_SCALE / jnp.sqrt(jnp.mean(data_gram * data_gram) + EPSILON)
    mixing = -step_size * (data_gram + prior_gram) + jnp.sqrt(2.0 * step_size / ensemble) * noise

    updated = flat + dot32("kj,kc->jc", mixing, deviation)
    returned = lax.all_to_all(
        updated.reshape(owners, members_here, rows, columns),
        "mem",
        split_axis=0,
        concat_axis=0,
        tiled=True,
    )
    new_field = returned.transpose(1, 0, 2, 3).reshape(
        members_here, slab_width, levels, columns
    )
    mixing_rows = lax.dynamic_slice_in_dim(
        mixing, lax.axis_index("mem") * members_here, members_here, 0
    )
    return (new_field, predicted, mixing_rows)


def solution(mesh):
    in_specs = (
        P(("grp", "mem"), "slab", None, None),
        P(("grp", "slab"), None, None),
        P(("grp", "slab")),
        P(("grp", "slab")),
        P(("grp", "slab")),
        P("grp", None),
    )
    out_specs = (
        P(("grp", "mem"), "slab", None, None),
        P(("grp", "mem"), "slab"),
        P(("grp", "mem"), None),
    )
    return jax.shard_map(
        per_device, mesh=mesh, in_specs=in_specs, out_specs=out_specs, check_vma=False
    )
```

```python
import functools

import jax
import jax.numpy as jnp
from jax import lax
from jax.experimental import pallas as pl
from jax.experimental.pallas import tpu as pltpu
from jax.sharding import PartitionSpec as P

STEPS = 3

ADVECT_SPEED = 0.1
KAPPA_BASE = 0.07
KAPPA_SWING = 0.05
STEP_SCALE = 0.02
PRIOR_VARIANCE = 0.02
EPSILON = 1e-06

LANES = 128
SUBLANES = 8

VMEM = pl.BlockSpec(memory_space=pltpu.VMEM)
SMEM = pl.BlockSpec(memory_space=pltpu.SMEM)
SMALL = pltpu.CompilerParams(vmem_limit_bytes=20 * 2**20)


def ring(axis):
    count = lax.axis_size(axis)
    forward = [(i, (i + 1) % count) for i in range(count)]
    backward = [(target, source) for source, target in forward]
    return forward, backward


def face_flux(left, right):
    mean_flux = 0.5 * (0.5 * ADVECT_SPEED * left * left + 0.5 * ADVECT_SPEED * right * right)
    speed = ADVECT_SPEED * jnp.maximum(jnp.abs(left), jnp.abs(right))
    return mean_flux - 0.5 * speed * (right - left)


def laplacian(below, center, above, first_level, last_level):
    levels, columns = center.shape
    upper = jnp.where(last_level, center, pltpu.roll(center, levels - 1, 0))
    lower = jnp.where(first_level, center, pltpu.roll(center, 1, 0))
    return (
        above
        + below
        + upper
        + lower
        + pltpu.roll(center, 1, 1)
        + pltpu.roll(center, columns - 1, 1)
        - 6.0 * center
    )


def forward_kernel(
    row_ref,
    turn_ref,
    tracer_ref,
    param_ref,
    low_ref,
    high_ref,
    out_ref,
    seen_ref,
    ext,
    kappa,
    buf_a,
    buf_b,
    table,
):
    members, width, levels, columns = param_ref.shape
    rim = STEPS - 1
    halves = columns // LANES
    pitch = SUBLANES
    row = lax.broadcasted_iota(jnp.int32, (levels, columns), 0)
    first_level = row == 0
    last_level = row == levels - 1

    for i in range(STEPS):
        ext[i] = low_ref[i]
        ext[STEPS + width + i] = high_ref[i]

    @pl.loop(0, width)
    def _(i):
        ext[STEPS + i] = tracer_ref[i]
        for m in range(members):
            kappa[m, rim + i] = KAPPA_BASE + KAPPA_SWING * jnp.tanh(param_ref[m, i])

    for m in range(members):
        for i in range(rim):
            at = STEPS + m * rim + i
            kappa[m, i] = KAPPA_BASE + KAPPA_SWING * jnp.tanh(low_ref[at])
            kappa[m, rim + width + i] = KAPPA_BASE + KAPPA_SWING * jnp.tanh(high_ref[at])

    def step_first(i, carry):
        below, center, flux_low = carry
        above = ext[i + 2]
        flux_high = face_flux(center, above)
        lap = laplacian(below, center, above, first_level, last_level)
        base = center - (flux_high - flux_low)
        for m in range(members):
            buf_a[m, i] = base + kappa[m, i] * lap
        return center, above, flux_high

    lax.fori_loop(
        0, width + 2 * rim, step_first, (ext[0], ext[1], face_flux(ext[0], ext[1]))
    )

    for number in range(1, STEPS):
        source, target = (buf_a, buf_b) if number % 2 else (buf_b, buf_a)
        margin = STEPS - 1 - number
        last = number == STEPS - 1
        for m in range(members):

            def step_next(i, carry):
                below, center, flux_low = carry
                above = source[m, i + 2]
                flux_high = face_flux(center, above)
                lap = laplacian(below, center, above, first_level, last_level)
                new = center - (flux_high - flux_low) + kappa[m, i + number] * lap
                if last:
                    for h in range(halves):
                        at = i * (levels * halves * pitch) + h * pitch + m
                        table[pl.ds(at, levels, stride=halves * pitch), :] = new[
                            :, h * LANES : (h + 1) * LANES
                        ]
                else:
                    target[m, i] = new
                return center, above, flux_high

            start = (source[m, 0], source[m, 1], face_flux(source[m, 0], source[m, 1]))
            lax.fori_loop(0, width + 2 * margin, step_next, start)

    lane = lax.broadcasted_iota(jnp.int32, (SUBLANES, LANES), 1)
    groups = out_ref.shape[1] // LANES

    @pl.loop(0, groups)
    def _(group):
        first = group * LANES
        picked = jnp.zeros((SUBLANES, LANES), jnp.float32)
        for o in range(LANES):
            at = pl.multiple_of(row_ref[first + o], pitch)
            rows = pltpu.roll(table[pl.ds(at, SUBLANES), :], turn_ref[first + o], 1)
            picked = jnp.where(lane == o, rows, picked)
        out_ref[:, pl.ds(pl.multiple_of(first, LANES), LANES)] = picked[:members]
        for m in range(members):
            seen_ref[pl.ds(m * groups + group, 1), :] = picked[m : m + 1]


def forward_observe(index, tracer, param, low, high):
    members, width, levels, columns = param.shape
    count = index.shape[0]
    rim = STEPS - 1
    rows = width * levels * (columns // LANES) * SUBLANES
    cell = index - lax.axis_index("slab") * (width * levels * columns)
    table_row = (cell // LANES) * SUBLANES
    turn = (jnp.arange(count, dtype=jnp.int32) - cell) % LANES
    return pl.pallas_call(
        forward_kernel,
        out_shape=(
            jax.ShapeDtypeStruct((members, count), jnp.float32),
            jax.ShapeDtypeStruct((members * count // LANES, LANES), jnp.float32),
        ),
        in_specs=[SMEM, SMEM, VMEM, VMEM, VMEM, VMEM],
        out_specs=(VMEM, VMEM),
        scratch_shapes=[
            pltpu.VMEM((width + 2 * STEPS, levels, columns), jnp.float32),
            pltpu.VMEM((members, width + 2 * rim, levels, columns), jnp.float32),
            pltpu.VMEM((members, width + 2 * rim, levels, columns), jnp.float32),
            pltpu.VMEM((members, width + 2 * rim, levels, columns), jnp.float32),
            pltpu.VMEM((rows, LANES), jnp.float32),
        ],
        cost_estimate=pl.CostEstimate(
            flops=100 * param.size, bytes_accessed=16 * param.size, transcendentals=param.size
        ),
        compiler_params=SMALL,
        name="forward_observe",
    )(table_row, turn, tracer, param, low, high)


def gram_kernel(owners, seen_ref, *refs):
    blocks = refs[:owners]
    dev_ref, mean_ref, load_ref = refs[owners:]
    members, rows, columns = blocks[0].shape
    ensemble = owners * members
    me = lax.axis_index("mem")

    @pl.loop(0, rows // SUBLANES)
    def _(r):
        at = pl.ds(pl.multiple_of(r * SUBLANES, SUBLANES), SUBLANES)
        parts = [blocks[b][m, at, :] for b in range(owners) for m in range(members)]
        total = parts[0]
        for part in parts[1:]:
            total = total + part
        mean = total * (1.0 / ensemble)
        mean_ref[at, :] = mean
        for b in range(owners):
            for m in range(members):
                dev_ref[(me ^ b) * members + m, at, :] = parts[b * members + m] - mean

    row = lax.broadcasted_iota(jnp.int32, (SUBLANES, LANES), 0)
    lane = lax.broadcasted_iota(jnp.int32, (SUBLANES, LANES), 1)

    def fold(left, right):
        product = left * right
        while product.shape[0] > SUBLANES:
            cut = product.shape[0] // 2
            product = product[:cut] + product[cut:]
        total = product[:, :LANES]
        for h in range(1, columns // LANES):
            total = total + product[:, h * LANES : (h + 1) * LANES]
        return jnp.sum(total, axis=0, keepdims=True)

    packed = jnp.zeros((SUBLANES, LANES), jnp.float32)
    means = mean_ref[...]
    for k in range(ensemble):
        left = dev_ref[k]
        shift = jnp.sum(fold(left, means), axis=1, keepdims=True)
        sums = [fold(left, dev_ref[j]) for j in range(k + 1)]
        for first in range(0, k + 1, SUBLANES):
            stack = jnp.zeros((SUBLANES, LANES), jnp.float32)
            for j in range(first, min(first + SUBLANES, k + 1)):
                stack = jnp.where(row == j - first, sums[j], stack)
            column = jnp.sum(stack, axis=1, keepdims=True)
            packed = jnp.where(lane == first // SUBLANES * ensemble + k, column, packed)
        packed = jnp.where(
            (lane == 2 * ensemble) & (row == k % SUBLANES) if k < SUBLANES
            else (lane == 2 * ensemble + 1) & (row == k % SUBLANES),
            shift,
            packed,
        )
    lines = seen_ref.shape[0]
    for b in range(owners):
        load_ref[b, :lines] = seen_ref[...]
        load_ref[b, lines:] = packed


def gram_call(seen, blocks):
    owners = len(blocks)
    members, rows, columns = blocks[0].shape
    ensemble = owners * members
    lines = seen.shape[0] + SUBLANES
    return pl.pallas_call(
        functools.partial(gram_kernel, owners),
        out_shape=(
            jax.ShapeDtypeStruct((ensemble, rows, columns), jnp.float32),
            jax.ShapeDtypeStruct((rows, columns), jnp.float32),
            jax.ShapeDtypeStruct((owners, lines, LANES), jnp.float32),
        ),
        in_specs=[VMEM] * (owners + 1),
        out_specs=(VMEM,) * 3,
        compiler_params=SMALL,
        name="prior_products",
    )(seen, *blocks)


def unpack_products(packed, ensemble):
    upper = jnp.concatenate(
        [packed[:, i * ensemble : (i + 1) * ensemble] for i in range(ensemble // SUBLANES)], axis=0
    )
    upper = jnp.triu(upper)
    shift = jnp.concatenate(
        [packed[:, 2 * ensemble + i] for i in range(ensemble // SUBLANES)], axis=0
    )
    return upper + jnp.triu(upper, 1).T + shift[:, None]


def mix_kernel(
    total_cells, order, own_ref, other_ref, noise_ref, dev_ref, mean_ref, *refs
):
    outs = refs[: len(order)]
    rows_ref, coef = refs[len(order) :]
    ensemble, rows, columns = dev_ref.shape
    members = outs[0].shape[0]
    me = lax.axis_index("mem")

    data_gram = (own_ref[0] + other_ref[0]) * (1.0 / ensemble)
    prior_gram = (own_ref[1] + other_ref[1]) * (
        1.0 / (ensemble * PRIOR_VARIANCE * total_cells)
    )
    power = jnp.sum(data_gram * data_gram, keepdims=True) / (ensemble * ensemble)
    step_size = STEP_SCALE / jnp.sqrt(power + EPSILON)
    mixing = (
        -step_size * (data_gram + prior_gram)
        + jnp.sqrt(2.0 * step_size / ensemble) * noise_ref[...]
    )
    rows_ref[...] = mixing
    weight = mixing + jnp.where(
        lax.broadcasted_iota(jnp.int32, mixing.shape, 0)
        == lax.broadcasted_iota(jnp.int32, mixing.shape, 1),
        1.0,
        0.0,
    )
    for j in range(ensemble):
        coef[j] = jnp.broadcast_to(weight[:, j : j + 1], (ensemble, LANES))

    for out, b in zip(outs, order):
        for m in range(members):
            j = (me ^ b) * members + m

            @pl.loop(0, rows // (2 * SUBLANES))
            def _(r):
                at = pl.ds(pl.multiple_of(r * 2 * SUBLANES, 2 * SUBLANES), 2 * SUBLANES)
                total = mean_ref[at, :]
                for k in range(ensemble):
                    scale = jnp.broadcast_to(coef[j, k : k + 1, :], (2 * SUBLANES, LANES))
                    scale = jnp.concatenate([scale] * (columns // LANES), axis=1)
                    total = total + scale * dev_ref[k, at, :]
                out[m, at, :] = total


def mix_call(own, other, noise, dev, mean, total_cells, order):
    ensemble, rows, columns = dev.shape
    members = ensemble // lax.axis_size("mem")
    block = jax.ShapeDtypeStruct((members, rows, columns), jnp.float32)
    result = pl.pallas_call(
        functools.partial(mix_kernel, total_cells, order),
        out_shape=(block,) * len(order)
        + (jax.ShapeDtypeStruct((ensemble, ensemble), jnp.float32),),
        in_specs=[VMEM] * 5,
        out_specs=(VMEM,) * (len(order) + 1),
        scratch_shapes=[pltpu.VMEM((ensemble, ensemble, LANES), jnp.float32)],
        compiler_params=SMALL,
        name="mix_update",
    )(own, other, noise, dev, mean)
    return result[:-1], result[-1]


def cut_kernel(owners, tracer_ref, param_ref, *refs):
    blocks = refs[:owners]
    to_high, to_low, sem = refs[owners:]
    members, width = param_ref.shape[:2]
    rim = STEPS - 1
    me = lax.axis_index("mem")
    flat = param_ref.reshape(members, width * param_ref.shape[2], param_ref.shape[3])
    rows = blocks[0].shape[1]
    copies = []
    for b in range(owners):
        at = pl.ds(pl.multiple_of((me ^ b) * rows, rows), rows)
        copies.append((flat.at[:, at], blocks[b]))
    copies.append((tracer_ref.at[pl.ds(width - STEPS, STEPS)], to_high.at[pl.ds(0, STEPS)]))
    copies.append((tracer_ref.at[pl.ds(0, STEPS)], to_low.at[pl.ds(0, STEPS)]))
    for m in range(members):
        at = pl.ds(STEPS + m * rim, rim)
        copies.append((param_ref.at[m, pl.ds(width - rim, rim)], to_high.at[at]))
        copies.append((param_ref.at[m, pl.ds(0, rim)], to_low.at[at]))
    started = [
        pltpu.make_async_copy(source, target, sem.at[i])
        for i, (source, target) in enumerate(copies)
    ]
    for copy in started:
        copy.start()
    for copy in started:
        copy.wait()


def cut_call(tracer, param, owners):
    members, width, levels, columns = param.shape
    rim = STEPS - 1
    block = jax.ShapeDtypeStruct((members, width * levels // owners, columns), jnp.float32)
    edge = jax.ShapeDtypeStruct((STEPS + members * rim, levels, columns), jnp.float32)
    result = pl.pallas_call(
        functools.partial(cut_kernel, owners),
        out_shape=(block,) * owners + (edge, edge),
        in_specs=[pl.BlockSpec(memory_space=pl.ANY)] * 2,
        out_specs=(VMEM,) * (owners + 2),
        scratch_shapes=[pltpu.SemaphoreType.DMA((owners + 2 + 2 * members,))],
        compiler_params=SMALL,
        name="cut_blocks",
    )(tracer, param)
    return result[:owners], result[owners], result[owners + 1]


def join_kernel(owners, *refs):
    blocks = refs[:owners]
    out_ref, sem = refs[owners:]
    me = lax.axis_index("mem")
    rows = blocks[0].shape[1]
    started = []
    for b in range(owners):
        at = pl.ds(pl.multiple_of((me ^ b) * rows, rows), rows)
        started.append(pltpu.make_async_copy(blocks[b], out_ref.at[:, at], sem.at[b]))
    for copy in started:
        copy.start()
    for copy in started:
        copy.wait()


def join_call(blocks):
    owners = len(blocks)
    members, rows, columns = blocks[0].shape
    return pl.pallas_call(
        functools.partial(join_kernel, owners),
        out_shape=jax.ShapeDtypeStruct((members, owners * rows, columns), jnp.float32),
        in_specs=[VMEM] * owners,
        out_specs=pl.BlockSpec(memory_space=pl.ANY),
        scratch_shapes=[pltpu.SemaphoreType.DMA((owners,))],
        compiler_params=SMALL,
        name="join_blocks",
    )(*blocks)


def dot32(spec, a, b):
    return jnp.einsum(
        spec, a, b, precision=lax.Precision.HIGHEST, preferred_element_type=jnp.float32
    )


def swap(block, b):
    count = lax.axis_size("mem")
    return lax.ppermute(block, "mem", [(i, i ^ b) for i in range(count)])


def data_products(values, observed, variance):
    spread = values - jnp.mean(values, axis=0, keepdims=True)
    weighted = (values - observed[None]) / variance[None]
    return dot32("ko,jo->kj", spread, weighted)


def broadcast_exchange(load):
    return lax.all_to_all(load, "mem", split_axis=0, concat_axis=0, tiled=True)


def small_ensemble(
    parameter_field, initial_tracer, observed, observation_variance, observation_index, noise
):
    members_here, slab_width, levels, columns = parameter_field.shape
    ensemble = noise.shape[0]
    owners = lax.axis_size("mem")
    total_cells = slab_width * levels * columns * lax.axis_size("slab")

    blocks, to_high, to_low = cut_call(initial_tracer, parameter_field, owners)
    forward, backward = ring("slab")
    low = lax.ppermute(to_high, "slab", forward)
    high = lax.ppermute(to_low, "slab", backward)
    near = [blocks[0]] + [swap(blocks[b], b) for b in range(1, owners)]

    predicted, seen = forward_observe(
        observation_index, initial_tracer, parameter_field, low, high
    )
    dev, mean, load = gram_call(seen, near)
    everyone = broadcast_exchange(load)
    cut = seen.shape[0]
    values = everyone[:, :cut].reshape(ensemble, -1)
    data_part = data_products(values, observed, observation_variance)
    prior_part = unpack_products(jnp.sum(everyone[:, cut:], axis=0), ensemble)
    own = jnp.stack([data_part, prior_part])
    other = sum_of_others(own)

    order = tuple(range(owners - 1, -1, -1))
    sent, mixing = mix_call(own, other, noise, dev, mean, total_cells, order)
    back = [None] * owners
    for b, block in zip(order, sent):
        back[b] = swap(block, b) if b else block
    new_field = join_call(back).reshape(parameter_field.shape)
    mixing_rows = lax.dynamic_slice_in_dim(
        mixing, lax.axis_index("mem") * members_here, members_here, 0
    )
    return (new_field, predicted, mixing_rows)


def sum_of_others(own):
    count = lax.axis_size("slab")
    forward, _ = ring("slab")
    total, moving = None, own
    for _ in range(count - 1):
        moving = lax.ppermute(moving, "slab", forward)
        total = moving if total is None else total + moving
    return jnp.zeros_like(own) if total is None else total


def large_ensemble(
    parameter_field, initial_tracer, observed, observation_variance, observation_index, noise
):
    members_here, slab_width, levels, columns = parameter_field.shape
    ensemble = noise.shape[0]
    owners = lax.axis_size("mem")
    cell_rows = slab_width * levels
    rows = cell_rows // owners
    total_cells = cell_rows * columns * lax.axis_size("slab")
    rim = STEPS - 1

    forward, backward = ring("slab")
    side = (members_here * rim, levels, columns)
    to_high = jnp.concatenate(
        [initial_tracer[-STEPS:], parameter_field[:, -rim:].reshape(side)], axis=0
    )
    to_low = jnp.concatenate(
        [initial_tracer[:STEPS], parameter_field[:, :rim].reshape(side)], axis=0
    )
    low = lax.ppermute(to_high, "slab", forward)
    high = lax.ppermute(to_low, "slab", backward)

    blocks = parameter_field.reshape(members_here, owners, rows, columns).transpose(1, 0, 2, 3)
    near = lax.all_to_all(blocks, "mem", split_axis=0, concat_axis=0, tiled=True)
    predicted, _ = forward_observe(
        observation_index, initial_tracer, parameter_field, low, high
    )
    flat = near.reshape(ensemble, rows * columns)
    deviation = flat - jnp.mean(flat, axis=0, keepdims=True)
    prior_part = dot32("kc,jc->kj", deviation, flat)

    values = lax.all_gather(predicted, "mem", axis=0, tiled=True)
    data_part = data_products(values, observed, observation_variance)
    data_gram = lax.psum(data_part, "slab") / ensemble
    prior_gram = lax.psum(prior_part, ("mem", "slab")) / (
        ensemble * PRIOR_VARIANCE * total_cells
    )
    step_size = STEP_SCALE / jnp.sqrt(jnp.mean(data_gram * data_gram) + EPSILON)
    mixing = -step_size * (data_gram + prior_gram) + jnp.sqrt(2.0 * step_size / ensemble) * noise
    updated = flat + dot32("kj,kc->jc", mixing, deviation)
    returned = lax.all_to_all(
        updated.reshape(owners, members_here, rows, columns),
        "mem",
        split_axis=0,
        concat_axis=0,
        tiled=True,
    )
    new_field = returned.transpose(1, 0, 2, 3).reshape(parameter_field.shape)
    mixing_rows = lax.dynamic_slice_in_dim(
        mixing, lax.axis_index("mem") * members_here, members_here, 0
    )
    return (new_field, predicted, mixing_rows)


def per_device(*arrays):
    owners = lax.axis_size("mem")
    ensemble = arrays[-1].shape[0]
    swaps = owners > 1 and owners & (owners - 1) == 0 and ensemble % SUBLANES == 0
    if swaps and ensemble <= 2 * SUBLANES:
        return small_ensemble(*arrays)
    return large_ensemble(*arrays)


def solution(mesh):
    in_specs = (
        P(("grp", "mem"), "slab", None, None),
        P(("grp", "slab"), None, None),
        P(("grp", "slab")),
        P(("grp", "slab")),
        P(("grp", "slab")),
        P("grp", None),
    )
    out_specs = (
        P(("grp", "mem"), "slab", None, None),
        P(("grp", "mem"), "slab"),
        P(("grp", "mem"), None),
    )
    return jax.shard_map(
        per_device, mesh=mesh, in_specs=in_specs, out_specs=out_specs, check_vma=False
    )
```

```python
import functools

import jax
import jax.numpy as jnp
from jax import lax
from jax.experimental import pallas as pl
from jax.experimental.pallas import tpu as pltpu
from jax.sharding import PartitionSpec as P

STEPS = 3

ADVECT_SPEED = 0.1
KAPPA_BASE = 0.07
KAPPA_SWING = 0.05
STEP_SCALE = 0.02
PRIOR_VARIANCE = 0.02
EPSILON = 1e-06

LANES = 128
SUBLANES = 8

VMEM = pl.BlockSpec(memory_space=pltpu.VMEM)
SMEM = pl.BlockSpec(memory_space=pltpu.SMEM)
SMALL = pltpu.CompilerParams(vmem_limit_bytes=20 * 2**20)


def ring(axis):
    count = lax.axis_size(axis)
    forward = [(i, (i + 1) % count) for i in range(count)]
    backward = [(target, source) for source, target in forward]
    return forward, backward


def face_flux(left, right):
    mean_flux = 0.5 * (0.5 * ADVECT_SPEED * left * left + 0.5 * ADVECT_SPEED * right * right)
    speed = ADVECT_SPEED * jnp.maximum(jnp.abs(left), jnp.abs(right))
    return mean_flux - 0.5 * speed * (right - left)


def laplacian(below, center, above, first_level, last_level):
    levels, columns = center.shape
    upper = jnp.where(last_level, center, pltpu.roll(center, levels - 1, 0))
    lower = jnp.where(first_level, center, pltpu.roll(center, 1, 0))
    return (
        above
        + below
        + upper
        + lower
        + pltpu.roll(center, 1, 1)
        + pltpu.roll(center, columns - 1, 1)
        - 6.0 * center
    )


def forward_kernel(
    row_ref,
    turn_ref,
    tracer_ref,
    param_ref,
    low_ref,
    high_ref,
    observed_ref,
    variance_ref,
    out_ref,
    seen_ref,
    target_ref,
    weight_ref,
    ext,
    kappa,
    buf_a,
    buf_b,
    table,
):
    members, width, levels, columns = param_ref.shape
    rim = STEPS - 1
    halves = columns // LANES
    pitch = SUBLANES
    row = lax.broadcasted_iota(jnp.int32, (levels, columns), 0)
    first_level = row == 0
    last_level = row == levels - 1

    target_ref[...] = observed_ref[...]
    weight_ref[...] = variance_ref[...]
    for i in range(STEPS):
        ext[i] = low_ref[i]
        ext[STEPS + width + i] = high_ref[i]

    @pl.loop(0, width)
    def _(i):
        ext[STEPS + i] = tracer_ref[i]
        for m in range(members):
            kappa[m, rim + i] = KAPPA_BASE + KAPPA_SWING * jnp.tanh(param_ref[m, i])

    for m in range(members):
        for i in range(rim):
            at = STEPS + m * rim + i
            kappa[m, i] = KAPPA_BASE + KAPPA_SWING * jnp.tanh(low_ref[at])
            kappa[m, rim + width + i] = KAPPA_BASE + KAPPA_SWING * jnp.tanh(high_ref[at])

    def step_first(i, carry):
        below, center, flux_low = carry
        above = ext[i + 2]
        flux_high = face_flux(center, above)
        lap = laplacian(below, center, above, first_level, last_level)
        base = center - (flux_high - flux_low)
        for m in range(members):
            buf_a[m, i] = base + kappa[m, i] * lap
        return center, above, flux_high

    lax.fori_loop(
        0, width + 2 * rim, step_first, (ext[0], ext[1], face_flux(ext[0], ext[1]))
    )

    for number in range(1, STEPS):
        source, target = (buf_a, buf_b) if number % 2 else (buf_b, buf_a)
        margin = STEPS - 1 - number
        last = number == STEPS - 1
        for m in range(members):

            def step_next(i, carry):
                below, center, flux_low = carry
                above = source[m, i + 2]
                flux_high = face_flux(center, above)
                lap = laplacian(below, center, above, first_level, last_level)
                new = center - (flux_high - flux_low) + kappa[m, i + number] * lap
                if last:
                    for h in range(halves):
                        at = i * (levels * halves * pitch) + h * pitch + m
                        table[pl.ds(at, levels, stride=halves * pitch), :] = new[
                            :, h * LANES : (h + 1) * LANES
                        ]
                else:
                    target[m, i] = new
                return center, above, flux_high

            start = (source[m, 0], source[m, 1], face_flux(source[m, 0], source[m, 1]))
            lax.fori_loop(0, width + 2 * margin, step_next, start)

    lane = lax.broadcasted_iota(jnp.int32, (SUBLANES, LANES), 1)
    groups = out_ref.shape[1] // LANES

    @pl.loop(0, groups)
    def _(group):
        first = group * LANES
        picked = jnp.zeros((SUBLANES, LANES), jnp.float32)
        for o in range(LANES):
            at = pl.multiple_of(row_ref[first + o], pitch)
            rows = pltpu.roll(table[pl.ds(at, SUBLANES), :], turn_ref[first + o], 1)
            picked = jnp.where(lane == o, rows, picked)
        out_ref[:, pl.ds(pl.multiple_of(first, LANES), LANES)] = picked[:members]
        for m in range(members):
            seen_ref[pl.ds(m * groups + group, 1), :] = picked[m : m + 1]


def forward_observe(index, tracer, param, low, high, observed, variance):
    members, width, levels, columns = param.shape
    count = index.shape[0]
    rim = STEPS - 1
    rows = width * levels * (columns // LANES) * SUBLANES
    cell = index - lax.axis_index("slab") * (width * levels * columns)
    table_row = (cell // LANES) * SUBLANES
    turn = (jnp.arange(count, dtype=jnp.int32) - cell) % LANES
    return pl.pallas_call(
        forward_kernel,
        out_shape=(
            jax.ShapeDtypeStruct((members, count), jnp.float32),
            jax.ShapeDtypeStruct((members * count // LANES, LANES), jnp.float32),
            jax.ShapeDtypeStruct((count // LANES, LANES), jnp.float32),
            jax.ShapeDtypeStruct((count // LANES, LANES), jnp.float32),
        ),
        in_specs=[SMEM, SMEM] + [VMEM] * 6,
        out_specs=(VMEM,) * 4,
        scratch_shapes=[
            pltpu.VMEM((width + 2 * STEPS, levels, columns), jnp.float32),
            pltpu.VMEM((members, width + 2 * rim, levels, columns), jnp.float32),
            pltpu.VMEM((members, width + 2 * rim, levels, columns), jnp.float32),
            pltpu.VMEM((members, width + 2 * rim, levels, columns), jnp.float32),
            pltpu.VMEM((rows, LANES), jnp.float32),
        ],
        cost_estimate=pl.CostEstimate(
            flops=100 * param.size, bytes_accessed=16 * param.size, transcendentals=param.size
        ),
        compiler_params=SMALL,
        name="forward_observe",
    )(
        table_row,
        turn,
        tracer,
        param,
        low,
        high,
        observed.reshape(-1, LANES),
        variance.reshape(-1, LANES),
    )


def gram_kernel(order, seen_ref, *refs):
    owners = len(order)
    blocks = refs[:owners]
    dev_ref, mean_ref, load_ref = refs[owners:]
    members, rows, columns = blocks[0].shape
    ensemble = owners * members
    me = lax.axis_index("mem")

    @pl.loop(0, rows // SUBLANES)
    def _(r):
        at = pl.ds(pl.multiple_of(r * SUBLANES, SUBLANES), SUBLANES)
        parts = [blocks[b][m, at, :] for b in range(owners) for m in range(members)]
        total = parts[0]
        for part in parts[1:]:
            total = total + part
        mean = total * (1.0 / ensemble)
        mean_ref[at, :] = mean
        for i, b in enumerate(order):
            for m in range(members):
                dev_ref[(me ^ b) * members + m, at, :] = parts[i * members + m] - mean

    row = lax.broadcasted_iota(jnp.int32, (SUBLANES, LANES), 0)
    lane = lax.broadcasted_iota(jnp.int32, (SUBLANES, LANES), 1)

    def fold(left, right):
        product = left * right
        while product.shape[0] > SUBLANES:
            cut = product.shape[0] // 2
            product = product[:cut] + product[cut:]
        total = product[:, :LANES]
        for h in range(1, columns // LANES):
            total = total + product[:, h * LANES : (h + 1) * LANES]
        return jnp.sum(total, axis=0, keepdims=True)

    packed = jnp.zeros((SUBLANES, LANES), jnp.float32)
    means = mean_ref[...]
    for k in range(ensemble):
        left = dev_ref[k]
        shift = jnp.sum(fold(left, means), axis=1, keepdims=True)
        sums = [fold(left, dev_ref[j]) for j in range(k + 1)]
        for first in range(0, k + 1, SUBLANES):
            stack = jnp.zeros((SUBLANES, LANES), jnp.float32)
            for j in range(first, min(first + SUBLANES, k + 1)):
                stack = jnp.where(row == j - first, sums[j], stack)
            column = jnp.sum(stack, axis=1, keepdims=True)
            packed = jnp.where(lane == first // SUBLANES * ensemble + k, column, packed)
        packed = jnp.where(
            (lane == 2 * ensemble) & (row == k % SUBLANES) if k < SUBLANES
            else (lane == 2 * ensemble + 1) & (row == k % SUBLANES),
            shift,
            packed,
        )
    lines = seen_ref.shape[0]
    for b in range(owners):
        load_ref[b, :lines] = seen_ref[...]
        load_ref[b, lines:] = packed


def gram_call(seen, blocks, order):
    owners = len(order)
    members, rows, columns = blocks[0].shape
    ensemble = owners * members
    lines = seen.shape[0] + SUBLANES
    return pl.pallas_call(
        functools.partial(gram_kernel, order),
        out_shape=(
            jax.ShapeDtypeStruct((ensemble, rows, columns), jnp.float32),
            jax.ShapeDtypeStruct((rows, columns), jnp.float32),
            jax.ShapeDtypeStruct((owners, lines, LANES), jnp.float32),
        ),
        in_specs=[VMEM] * (owners + 1),
        out_specs=(VMEM,) * 3,
        compiler_params=SMALL,
        name="prior_products",
    )(seen, *blocks)


def unpack_products(packed, ensemble):
    upper = jnp.concatenate(
        [packed[:, i * ensemble : (i + 1) * ensemble] for i in range(ensemble // SUBLANES)], axis=0
    )
    upper = jnp.triu(upper)
    shift = jnp.concatenate(
        [packed[:, 2 * ensemble + i] for i in range(ensemble // SUBLANES)], axis=0
    )
    return upper + jnp.triu(upper, 1).T + shift[:, None]


def mix_kernel(
    total_cells, order, own_ref, other_ref, noise_ref, dev_ref, mean_ref, *refs
):
    outs = refs[: len(order)]
    rows_ref, coef = refs[len(order) :]
    ensemble, rows, columns = dev_ref.shape
    members = outs[0].shape[0]
    me = lax.axis_index("mem")

    data_gram = (own_ref[0] + other_ref[0]) * (1.0 / ensemble)
    prior_gram = (own_ref[1] + other_ref[1]) * (
        1.0 / (ensemble * PRIOR_VARIANCE * total_cells)
    )
    power = jnp.sum(data_gram * data_gram, keepdims=True) / (ensemble * ensemble)
    step_size = STEP_SCALE / jnp.sqrt(power + EPSILON)
    mixing = (
        -step_size * (data_gram + prior_gram)
        + jnp.sqrt(2.0 * step_size / ensemble) * noise_ref[...]
    )
    rows_ref[...] = mixing
    weight = mixing + jnp.where(
        lax.broadcasted_iota(jnp.int32, mixing.shape, 0)
        == lax.broadcasted_iota(jnp.int32, mixing.shape, 1),
        1.0,
        0.0,
    )
    for j in range(ensemble):
        coef[j] = jnp.broadcast_to(weight[:, j : j + 1], (ensemble, LANES))

    for out, b in zip(outs, order):
        for m in range(members):
            j = (me ^ b) * members + m

            @pl.loop(0, rows // (2 * SUBLANES))
            def _(r):
                at = pl.ds(pl.multiple_of(r * 2 * SUBLANES, 2 * SUBLANES), 2 * SUBLANES)
                total = mean_ref[at, :]
                for k in range(ensemble):
                    scale = jnp.broadcast_to(coef[j, k : k + 1, :], (2 * SUBLANES, LANES))
                    scale = jnp.concatenate([scale] * (columns // LANES), axis=1)
                    total = total + scale * dev_ref[k, at, :]
                out[m, at, :] = total


def mix_call(own, other, noise, dev, mean, total_cells, order):
    ensemble, rows, columns = dev.shape
    members = ensemble // lax.axis_size("mem")
    block = jax.ShapeDtypeStruct((members, rows, columns), jnp.float32)
    result = pl.pallas_call(
        functools.partial(mix_kernel, total_cells, order),
        out_shape=(block,) * len(order)
        + (jax.ShapeDtypeStruct((ensemble, ensemble), jnp.float32),),
        in_specs=[VMEM] * 5,
        out_specs=(VMEM,) * (len(order) + 1),
        scratch_shapes=[pltpu.VMEM((ensemble, ensemble, LANES), jnp.float32)],
        compiler_params=SMALL,
        name="mix_update",
    )(own, other, noise, dev, mean)
    return result[:-1], result[-1]


def cut_blocks(param, owners):
    members, width, levels, columns = param.shape
    flat = param.reshape(members, width * levels, columns)
    rows = width * levels // owners
    me = lax.axis_index("mem")
    return [
        lax.dynamic_slice_in_dim(flat, (me ^ b) * rows, rows, axis=1) for b in range(owners)
    ]


def slab_rims(tracer, param):
    members, width, levels, columns = param.shape
    rim = STEPS - 1
    side = (members * rim, levels, columns)
    forward, backward = ring("slab")
    to_high = [tracer[-STEPS:], param[:, -rim:].reshape(side)]
    to_low = [tracer[:STEPS], param[:, :rim].reshape(side)]
    if forward == backward:
        moved = lax.ppermute(jnp.concatenate(to_high + to_low, axis=0), "slab", forward)
        return moved[: STEPS + members * rim], moved[STEPS + members * rim :]
    low = lax.ppermute(jnp.concatenate(to_high, axis=0), "slab", forward)
    high = lax.ppermute(jnp.concatenate(to_low, axis=0), "slab", backward)
    return low, high


def join_kernel(order, *refs):
    owners = len(order)
    blocks = refs[:owners]
    out_ref, sem = refs[owners:]
    me = lax.axis_index("mem")
    rows = blocks[0].shape[1]
    started = []
    for i, b in enumerate(order):
        at = pl.ds(pl.multiple_of((me ^ b) * rows, rows), rows)
        started.append(pltpu.make_async_copy(blocks[i], out_ref.at[:, at], sem.at[i]))
    for copy in started:
        copy.start()
    for copy in started:
        copy.wait()


def join_call(blocks, order):
    owners = len(blocks)
    members, rows, columns = blocks[0].shape
    return pl.pallas_call(
        functools.partial(join_kernel, order),
        out_shape=jax.ShapeDtypeStruct((members, owners * rows, columns), jnp.float32),
        in_specs=[VMEM] * owners,
        out_specs=pl.BlockSpec(memory_space=pl.ANY),
        scratch_shapes=[pltpu.SemaphoreType.DMA((owners,))],
        compiler_params=SMALL,
        name="join_blocks",
    )(*blocks)


def dot32(spec, a, b):
    return jnp.einsum(
        spec, a, b, precision=lax.Precision.HIGHEST, preferred_element_type=jnp.float32
    )


def far_first(owners):
    half = owners // 2
    return tuple(range(half, owners)) + tuple(range(1, half)) + (0,)


def swap(block, b):
    count = lax.axis_size("mem")
    return lax.ppermute(block, "mem", [(i, i ^ b) for i in range(count)])


def data_products(values, observed, variance):
    spread = values - jnp.mean(values, axis=0, keepdims=True)
    weighted = (values - observed[None]) / variance[None]
    return dot32("ko,jo->kj", spread, weighted)


def broadcast_exchange(load):
    return lax.all_to_all(load, "mem", split_axis=0, concat_axis=0, tiled=True)


def small_ensemble(
    parameter_field, initial_tracer, observed, observation_variance, observation_index, noise
):
    members_here, slab_width, levels, columns = parameter_field.shape
    ensemble = noise.shape[0]
    owners = lax.axis_size("mem")
    total_cells = slab_width * levels * columns * lax.axis_size("slab")

    low, high = slab_rims(initial_tracer, parameter_field)
    blocks = cut_blocks(parameter_field, owners)
    order = far_first(owners)
    near = [swap(blocks[b], b) for b in order[:-1]] + [blocks[0]]

    predicted, seen, target, spread = forward_observe(
        observation_index,
        initial_tracer,
        parameter_field,
        low,
        high,
        observed,
        observation_variance,
    )
    dev, mean, load = gram_call(seen, near, order)
    everyone = broadcast_exchange(load)
    cut = seen.shape[0]
    values = everyone[:, :cut].reshape(ensemble, -1)
    data_part = data_products(values, target.reshape(-1), spread.reshape(-1))
    prior_part = unpack_products(jnp.sum(everyone[:, cut:], axis=0), ensemble)
    own = jnp.stack([data_part, prior_part])
    other = sum_of_others(own)

    sent, mixing = mix_call(own, other, noise, dev, mean, total_cells, order)
    back = [swap(block, b) for b, block in zip(order[:-1], sent)] + [sent[-1]]
    new_field = join_call(back, order).reshape(parameter_field.shape)
    mixing_rows = lax.dynamic_slice_in_dim(
        mixing, lax.axis_index("mem") * members_here, members_here, 0
    )
    return (new_field, predicted, mixing_rows)


def sum_of_others(own):
    count = lax.axis_size("slab")
    forward, _ = ring("slab")
    total, moving = None, own
    for _ in range(count - 1):
        moving = lax.ppermute(moving, "slab", forward)
        total = moving if total is None else total + moving
    return jnp.zeros_like(own) if total is None else total


def large_ensemble(
    parameter_field, initial_tracer, observed, observation_variance, observation_index, noise
):
    members_here, slab_width, levels, columns = parameter_field.shape
    ensemble = noise.shape[0]
    owners = lax.axis_size("mem")
    cell_rows = slab_width * levels
    rows = cell_rows // owners
    total_cells = cell_rows * columns * lax.axis_size("slab")
    low, high = slab_rims(initial_tracer, parameter_field)
    blocks = parameter_field.reshape(members_here, owners, rows, columns).transpose(1, 0, 2, 3)
    near = lax.all_to_all(blocks, "mem", split_axis=0, concat_axis=0, tiled=True)
    predicted = forward_observe(
        observation_index,
        initial_tracer,
        parameter_field,
        low,
        high,
        observed,
        observation_variance,
    )[0]
    flat = near.reshape(ensemble, rows * columns)
    deviation = flat - jnp.mean(flat, axis=0, keepdims=True)
    prior_part = dot32("kc,jc->kj", deviation, flat)

    values = lax.all_gather(predicted, "mem", axis=0, tiled=True)
    data_part = data_products(values, observed, observation_variance)
    data_gram = lax.psum(data_part, "slab") / ensemble
    prior_gram = lax.psum(prior_part, ("mem", "slab")) / (
        ensemble * PRIOR_VARIANCE * total_cells
    )
    step_size = STEP_SCALE / jnp.sqrt(jnp.mean(data_gram * data_gram) + EPSILON)
    mixing = -step_size * (data_gram + prior_gram) + jnp.sqrt(2.0 * step_size / ensemble) * noise
    updated = flat + dot32("kj,kc->jc", mixing, deviation)
    returned = lax.all_to_all(
        updated.reshape(owners, members_here, rows, columns),
        "mem",
        split_axis=0,
        concat_axis=0,
        tiled=True,
    )
    new_field = returned.transpose(1, 0, 2, 3).reshape(parameter_field.shape)
    mixing_rows = lax.dynamic_slice_in_dim(
        mixing, lax.axis_index("mem") * members_here, members_here, 0
    )
    return (new_field, predicted, mixing_rows)


def per_device(*arrays):
    owners = lax.axis_size("mem")
    ensemble = arrays[-1].shape[0]
    swaps = owners > 1 and owners & (owners - 1) == 0 and ensemble % SUBLANES == 0
    if swaps and ensemble <= 2 * SUBLANES:
        return small_ensemble(*arrays)
    return large_ensemble(*arrays)


def solution(mesh):
    in_specs = (
        P(("grp", "mem"), "slab", None, None),
        P(("grp", "slab"), None, None),
        P(("grp", "slab")),
        P(("grp", "slab")),
        P(("grp", "slab")),
        P("grp", None),
    )
    out_specs = (
        P(("grp", "mem"), "slab", None, None),
        P(("grp", "mem"), "slab"),
        P(("grp", "mem"), None),
    )
    return jax.shard_map(
        per_device, mesh=mesh, in_specs=in_specs, out_specs=out_specs, check_vma=False
    )
```

```python
import functools

import jax
import jax.numpy as jnp
from jax import lax
from jax.experimental import pallas as pl
from jax.experimental.pallas import tpu as pltpu
from jax.sharding import PartitionSpec as P

STEPS = 3

ADVECT_SPEED = 0.1
KAPPA_BASE = 0.07
KAPPA_SWING = 0.05
STEP_SCALE = 0.02
PRIOR_VARIANCE = 0.02
EPSILON = 1e-06

LANES = 128
SUBLANES = 8

VMEM = pl.BlockSpec(memory_space=pltpu.VMEM)
SMEM = pl.BlockSpec(memory_space=pltpu.SMEM)
SMALL = pltpu.CompilerParams(vmem_limit_bytes=20 * 2**20)


def ring(axis):
    count = lax.axis_size(axis)
    forward = [(i, (i + 1) % count) for i in range(count)]
    backward = [(target, source) for source, target in forward]
    return forward, backward


def twice_flux(left, right):
    speed = jnp.maximum(jnp.abs(left), jnp.abs(right))
    return (left * left + right * right) - (speed + speed) * (right - left)


def level_shifts(center, row):
    count = center.shape[0] // SUBLANES
    tiles = [center[t * SUBLANES : (t + 1) * SUBLANES] for t in range(count)]
    down = [pltpu.roll(tile, SUBLANES - 1, 0) for tile in tiles]
    up = [pltpu.roll(tile, 1, 0) for tile in tiles]
    upper = [
        jnp.where(row == SUBLANES - 1, down[t + 1] if t + 1 < count else tiles[t], down[t])
        for t in range(count)
    ]
    lower = [jnp.where(row == 0, up[t - 1] if t else tiles[t], up[t]) for t in range(count)]
    return jnp.concatenate(upper, axis=0), jnp.concatenate(lower, axis=0)


def laplacian(below, center, above, row):
    columns = center.shape[1]
    upper, lower = level_shifts(center, row)
    return (
        above
        + below
        + upper
        + lower
        + pltpu.roll(center, 1, 1)
        + pltpu.roll(center, columns - 1, 1)
        - 6.0 * center
    )


def sweep(count, body, flux):
    if count % 2:
        return lax.fori_loop(0, count, body, flux)
    return lax.fori_loop(0, count // 2, lambda i, f: body(2 * i + 1, body(2 * i, f)), flux)


def forward_kernel(
    line_ref,
    index_ref,
    tracer_ref,
    param_ref,
    low_ref,
    high_ref,
    observed_ref,
    variance_ref,
    out_ref,
    seen_ref,
    target_ref,
    weight_ref,
    ext,
    kappa,
    buf_a,
    buf_b,
    table,
    stage,
):
    members, width, levels, columns = param_ref.shape
    rim = STEPS - 1
    halves = columns // LANES
    pitch = SUBLANES
    row = lax.broadcasted_iota(jnp.int32, (SUBLANES, columns), 0)

    target_ref[...] = observed_ref[...]
    weight_ref[...] = variance_ref[...]
    for i in range(STEPS):
        ext[i] = low_ref[i]
        ext[STEPS + width + i] = high_ref[i]

    @pl.loop(0, width)
    def _(i):
        ext[STEPS + i] = tracer_ref[i]
        for m in range(members):
            kappa[m, rim + i] = KAPPA_BASE + KAPPA_SWING * jnp.tanh(param_ref[m, i])

    for m in range(members):
        for i in range(rim):
            at = STEPS + m * rim + i
            kappa[m, i] = KAPPA_BASE + KAPPA_SWING * jnp.tanh(low_ref[at])
            kappa[m, rim + width + i] = KAPPA_BASE + KAPPA_SWING * jnp.tanh(high_ref[at])

    def step_first(i, flux_low):
        center, above = ext[i + 1], ext[i + 2]
        flux_high = twice_flux(center, above)
        lap = laplacian(ext[i], center, above, row)
        base = center - (0.25 * ADVECT_SPEED) * (flux_high - flux_low)
        for m in range(members):
            buf_a[m, i] = base + kappa[m, i] * lap
        return flux_high

    sweep(width + 2 * rim, step_first, twice_flux(ext[0], ext[1]))

    for number in range(1, STEPS):
        source, target = (buf_a, buf_b) if number % 2 else (buf_b, buf_a)
        margin = STEPS - 1 - number
        last = number == STEPS - 1
        for m in range(members):

            def step_next(i, flux_low):
                center, above = source[m, i + 1], source[m, i + 2]
                flux_high = twice_flux(center, above)
                lap = laplacian(source[m, i], center, above, row)
                new = (
                    center
                    - (0.25 * ADVECT_SPEED) * (flux_high - flux_low)
                    + kappa[m, i + number] * lap
                )
                if last:
                    for h in range(halves):
                        at = i * (levels * halves * pitch) + h * pitch + m
                        table[pl.ds(at, levels, stride=halves * pitch), :] = new[
                            :, h * LANES : (h + 1) * LANES
                        ]
                else:
                    target[m, i] = new
                return flux_high

            sweep(width + 2 * margin, step_next, twice_flux(source[m, 0], source[m, 1]))

    sublane = lax.broadcasted_iota(jnp.int32, (LANES, LANES), 0)
    groups = out_ref.shape[1] // LANES

    for group in range(groups):
        first = group * LANES
        base = group % 2 * members * LANES
        for o in range(LANES):
            at = pl.multiple_of(line_ref[first + o], pitch)
            stage[base + o * members : base + (o + 1) * members, :] = table[
                pl.ds(at, members), :
            ]
        wanted = sublane == (index_ref[group : group + 1, :] & (LANES - 1))
        for m in range(members):
            turned = stage[pl.ds(base + m, LANES, stride=members), :].T
            picked = jnp.sum(jnp.where(wanted, turned, 0.0), axis=0, keepdims=True)
            out_ref[m : m + 1, first : first + LANES] = picked
            seen_ref[m * groups + group : m * groups + group + 1, :] = picked


def forward_observe(index, tracer, param, low, high, observed, variance):
    members, width, levels, columns = param.shape
    count = index.shape[0]
    rim = STEPS - 1
    rows = width * levels * (columns // LANES) * SUBLANES
    cell = index - lax.axis_index("slab") * (width * levels * columns)
    return pl.pallas_call(
        forward_kernel,
        out_shape=(
            jax.ShapeDtypeStruct((members, count), jnp.float32),
            jax.ShapeDtypeStruct((members * count // LANES, LANES), jnp.float32),
            jax.ShapeDtypeStruct((count // LANES, LANES), jnp.float32),
            jax.ShapeDtypeStruct((count // LANES, LANES), jnp.float32),
        ),
        in_specs=[SMEM] + [VMEM] * 7,
        out_specs=(VMEM,) * 4,
        scratch_shapes=[
            pltpu.VMEM((width + 2 * STEPS, levels, columns), jnp.float32),
            pltpu.VMEM((members, width + 2 * rim, levels, columns), jnp.float32),
            pltpu.VMEM((members, width + 2 * rim, levels, columns), jnp.float32),
            pltpu.VMEM((members, width + 2 * rim, levels, columns), jnp.float32),
            pltpu.VMEM((rows, LANES), jnp.float32),
            pltpu.VMEM((2 * members * LANES, LANES), jnp.float32),
        ],
        cost_estimate=pl.CostEstimate(
            flops=100 * param.size, bytes_accessed=16 * param.size, transcendentals=param.size
        ),
        compiler_params=SMALL,
        name="forward_observe",
    )(
        lax.shift_right_logical(cell, 7) * SUBLANES,
        index.reshape(-1, LANES),
        tracer,
        param,
        low,
        high,
        observed.reshape(-1, LANES),
        variance.reshape(-1, LANES),
    )


def gram_kernel(order, seen_ref, *refs):
    owners = len(order)
    blocks = refs[:owners]
    dev_ref, mean_ref, load_ref = refs[owners:]
    members, rows, columns = blocks[0].shape
    ensemble = owners * members
    me = lax.axis_index("mem")

    @pl.loop(0, rows // SUBLANES)
    def _(r):
        at = pl.ds(pl.multiple_of(r * SUBLANES, SUBLANES), SUBLANES)
        parts = [blocks[b][m, at, :] for b in range(owners) for m in range(members)]
        total = parts[0]
        for part in parts[1:]:
            total = total + part
        mean = total * (1.0 / ensemble)
        mean_ref[at, :] = mean
        for i, b in enumerate(order):
            for m in range(members):
                dev_ref[(me ^ b) * members + m, at, :] = parts[i * members + m] - mean

    row = lax.broadcasted_iota(jnp.int32, (SUBLANES, LANES), 0)
    lane = lax.broadcasted_iota(jnp.int32, (SUBLANES, LANES), 1)

    def fold(left, right):
        product = left * right
        while product.shape[0] > SUBLANES:
            cut = product.shape[0] // 2
            product = product[:cut] + product[cut:]
        total = product[:, :LANES]
        for h in range(1, columns // LANES):
            total = total + product[:, h * LANES : (h + 1) * LANES]
        return jnp.sum(total, axis=0, keepdims=True)

    packed = jnp.zeros((SUBLANES, LANES), jnp.float32)
    means = mean_ref[...]
    for k in range(ensemble):
        left = dev_ref[k]
        shift = jnp.sum(fold(left, means), axis=1, keepdims=True)
        sums = [fold(left, dev_ref[j]) for j in range(k + 1)]
        for first in range(0, k + 1, SUBLANES):
            stack = jnp.zeros((SUBLANES, LANES), jnp.float32)
            for j in range(first, min(first + SUBLANES, k + 1)):
                stack = jnp.where(row == j - first, sums[j], stack)
            column = jnp.sum(stack, axis=1, keepdims=True)
            packed = jnp.where(lane == first // SUBLANES * ensemble + k, column, packed)
        packed = jnp.where(
            (lane == 2 * ensemble) & (row == k % SUBLANES) if k < SUBLANES
            else (lane == 2 * ensemble + 1) & (row == k % SUBLANES),
            shift,
            packed,
        )
    lines = seen_ref.shape[0]
    for b in range(owners):
        load_ref[b, :lines] = seen_ref[...]
        load_ref[b, lines:] = packed


def gram_call(seen, blocks, order):
    owners = len(order)
    members, rows, columns = blocks[0].shape
    ensemble = owners * members
    lines = seen.shape[0] + SUBLANES
    return pl.pallas_call(
        functools.partial(gram_kernel, order),
        out_shape=(
            jax.ShapeDtypeStruct((ensemble, rows, columns), jnp.float32),
            jax.ShapeDtypeStruct((rows, columns), jnp.float32),
            jax.ShapeDtypeStruct((owners, lines, LANES), jnp.float32),
        ),
        in_specs=[VMEM] * (owners + 1),
        out_specs=(VMEM,) * 3,
        compiler_params=SMALL,
        name="prior_products",
    )(seen, *blocks)


def unpack_products(packed, ensemble):
    upper = jnp.concatenate(
        [packed[:, i * ensemble : (i + 1) * ensemble] for i in range(ensemble // SUBLANES)], axis=0
    )
    upper = jnp.triu(upper)
    shift = jnp.concatenate(
        [packed[:, 2 * ensemble + i] for i in range(ensemble // SUBLANES)], axis=0
    )
    return upper + jnp.triu(upper, 1).T + shift[:, None]


def mix_kernel(
    total_cells, order, own_ref, other_ref, noise_ref, dev_ref, mean_ref, *refs
):
    outs = refs[: len(order)]
    rows_ref, coef = refs[len(order) :]
    ensemble, rows, columns = dev_ref.shape
    members = outs[0].shape[0]
    me = lax.axis_index("mem")

    data_gram = (own_ref[0] + other_ref[0]) * (1.0 / ensemble)
    prior_gram = (own_ref[1] + other_ref[1]) * (
        1.0 / (ensemble * PRIOR_VARIANCE * total_cells)
    )
    power = jnp.sum(data_gram * data_gram, keepdims=True) / (ensemble * ensemble)
    step_size = STEP_SCALE / jnp.sqrt(power + EPSILON)
    mixing = (
        -step_size * (data_gram + prior_gram)
        + jnp.sqrt(2.0 * step_size / ensemble) * noise_ref[...]
    )
    rows_ref[...] = mixing
    weight = mixing + jnp.where(
        lax.broadcasted_iota(jnp.int32, mixing.shape, 0)
        == lax.broadcasted_iota(jnp.int32, mixing.shape, 1),
        1.0,
        0.0,
    )
    for j in range(ensemble):
        coef[j] = jnp.broadcast_to(weight[:, j : j + 1], (ensemble, LANES))

    for out, b in zip(outs, order):
        for m in range(members):
            j = (me ^ b) * members + m

            @pl.loop(0, rows // (2 * SUBLANES))
            def _(r):
                at = pl.ds(pl.multiple_of(r * 2 * SUBLANES, 2 * SUBLANES), 2 * SUBLANES)
                total = mean_ref[at, :]
                for k in range(ensemble):
                    scale = jnp.broadcast_to(coef[j, k : k + 1, :], (2 * SUBLANES, LANES))
                    scale = jnp.concatenate([scale] * (columns // LANES), axis=1)
                    total = total + scale * dev_ref[k, at, :]
                out[m, at, :] = total


def mix_call(own, other, noise, dev, mean, total_cells, order):
    ensemble, rows, columns = dev.shape
    members = ensemble // lax.axis_size("mem")
    block = jax.ShapeDtypeStruct((members, rows, columns), jnp.float32)
    result = pl.pallas_call(
        functools.partial(mix_kernel, total_cells, order),
        out_shape=(block,) * len(order)
        + (jax.ShapeDtypeStruct((ensemble, ensemble), jnp.float32),),
        in_specs=[VMEM] * 5,
        out_specs=(VMEM,) * (len(order) + 1),
        scratch_shapes=[pltpu.VMEM((ensemble, ensemble, LANES), jnp.float32)],
        compiler_params=SMALL,
        name="mix_update",
    )(own, other, noise, dev, mean)
    return result[:-1], result[-1]


def cut_blocks(param, owners):
    members, width, levels, columns = param.shape
    flat = param.reshape(members, width * levels, columns)
    rows = width * levels // owners
    me = lax.axis_index("mem")
    return [
        lax.dynamic_slice_in_dim(flat, (me ^ b) * rows, rows, axis=1) for b in range(owners)
    ]


def slab_rims(tracer, param):
    members, width, levels, columns = param.shape
    rim = STEPS - 1
    side = (members * rim, levels, columns)
    forward, backward = ring("slab")
    to_high = [tracer[-STEPS:], param[:, -rim:].reshape(side)]
    to_low = [tracer[:STEPS], param[:, :rim].reshape(side)]
    if forward == backward:
        moved = lax.ppermute(jnp.concatenate(to_high + to_low, axis=0), "slab", forward)
        return moved[: STEPS + members * rim], moved[STEPS + members * rim :]
    low = lax.ppermute(jnp.concatenate(to_high, axis=0), "slab", forward)
    high = lax.ppermute(jnp.concatenate(to_low, axis=0), "slab", backward)
    return low, high


def join_kernel(order, *refs):
    owners = len(order)
    blocks = refs[:owners]
    out_ref, sem = refs[owners:]
    me = lax.axis_index("mem")
    rows = blocks[0].shape[1]
    started = []
    for i, b in enumerate(order):
        at = pl.ds(pl.multiple_of((me ^ b) * rows, rows), rows)
        started.append(pltpu.make_async_copy(blocks[i], out_ref.at[:, at], sem.at[i]))
    for copy in started:
        copy.start()
    for copy in started:
        copy.wait()


def join_call(blocks, order):
    owners = len(blocks)
    members, rows, columns = blocks[0].shape
    return pl.pallas_call(
        functools.partial(join_kernel, order),
        out_shape=jax.ShapeDtypeStruct((members, owners * rows, columns), jnp.float32),
        in_specs=[VMEM] * owners,
        out_specs=pl.BlockSpec(memory_space=pl.ANY),
        scratch_shapes=[pltpu.SemaphoreType.DMA((owners,))],
        compiler_params=SMALL,
        name="join_blocks",
    )(*blocks)


def dot32(spec, a, b):
    return jnp.einsum(
        spec, a, b, precision=lax.Precision.HIGHEST, preferred_element_type=jnp.float32
    )


def far_first(owners):
    half = owners // 2
    return (1,) + tuple(range(owners - 1, half - 1, -1)) + tuple(range(half - 1, 1, -1)) + (0,)


def swap(block, b):
    count = lax.axis_size("mem")
    return lax.ppermute(block, "mem", [(i, i ^ b) for i in range(count)])


def data_products(values, observed, variance):
    spread = values - jnp.mean(values, axis=0, keepdims=True)
    weighted = (values - observed[None]) / variance[None]
    return dot32("ko,jo->kj", spread, weighted)


def broadcast_exchange(load):
    return lax.all_to_all(load, "mem", split_axis=0, concat_axis=0, tiled=True)


def small_ensemble(
    parameter_field, initial_tracer, observed, observation_variance, observation_index, noise
):
    members_here, slab_width, levels, columns = parameter_field.shape
    ensemble = noise.shape[0]
    owners = lax.axis_size("mem")
    total_cells = slab_width * levels * columns * lax.axis_size("slab")

    low, high = slab_rims(initial_tracer, parameter_field)
    blocks = cut_blocks(parameter_field, owners)
    order = far_first(owners)
    near = [swap(blocks[b], b) for b in order[:-1]] + [blocks[0]]

    predicted, seen, target, spread = forward_observe(
        observation_index,
        initial_tracer,
        parameter_field,
        low,
        high,
        observed,
        observation_variance,
    )
    dev, mean, load = gram_call(seen, near, order)
    everyone = broadcast_exchange(load)
    cut = seen.shape[0]
    values = everyone[:, :cut].reshape(ensemble, -1)
    data_part = data_products(values, target.reshape(-1), spread.reshape(-1))
    prior_part = unpack_products(jnp.sum(everyone[:, cut:], axis=0), ensemble)
    own = jnp.stack([data_part, prior_part])
    other = sum_of_others(own)

    sent, mixing = mix_call(own, other, noise, dev, mean, total_cells, order)
    back = [swap(block, b) for b, block in zip(order[:-1], sent)] + [sent[-1]]
    new_field = join_call(back, order).reshape(parameter_field.shape)
    mixing_rows = lax.dynamic_slice_in_dim(
        mixing, lax.axis_index("mem") * members_here, members_here, 0
    )
    return (new_field, predicted, mixing_rows)


def sum_of_others(own):
    count = lax.axis_size("slab")
    forward, _ = ring("slab")
    total, moving = None, own
    for _ in range(count - 1):
        moving = lax.ppermute(moving, "slab", forward)
        total = moving if total is None else total + moving
    return jnp.zeros_like(own) if total is None else total


def large_ensemble(
    parameter_field, initial_tracer, observed, observation_variance, observation_index, noise
):
    members_here, slab_width, levels, columns = parameter_field.shape
    ensemble = noise.shape[0]
    owners = lax.axis_size("mem")
    cell_rows = slab_width * levels
    rows = cell_rows // owners
    total_cells = cell_rows * columns * lax.axis_size("slab")
    low, high = slab_rims(initial_tracer, parameter_field)
    blocks = parameter_field.reshape(members_here, owners, rows, columns).transpose(1, 0, 2, 3)
    near = lax.all_to_all(blocks, "mem", split_axis=0, concat_axis=0, tiled=True)
    predicted = forward_observe(
        observation_index,
        initial_tracer,
        parameter_field,
        low,
        high,
        observed,
        observation_variance,
    )[0]
    flat = near.reshape(ensemble, rows * columns)
    deviation = flat - jnp.mean(flat, axis=0, keepdims=True)
    prior_part = dot32("kc,jc->kj", deviation, flat)

    values = lax.all_gather(predicted, "mem", axis=0, tiled=True)
    data_part = data_products(values, observed, observation_variance)
    data_gram = lax.psum(data_part, "slab") / ensemble
    prior_gram = lax.psum(prior_part, ("mem", "slab")) / (
        ensemble * PRIOR_VARIANCE * total_cells
    )
    step_size = STEP_SCALE / jnp.sqrt(jnp.mean(data_gram * data_gram) + EPSILON)
    mixing = -step_size * (data_gram + prior_gram) + jnp.sqrt(2.0 * step_size / ensemble) * noise
    updated = flat + dot32("kj,kc->jc", mixing, deviation)
    returned = lax.all_to_all(
        updated.reshape(owners, members_here, rows, columns),
        "mem",
        split_axis=0,
        concat_axis=0,
        tiled=True,
    )
    new_field = returned.transpose(1, 0, 2, 3).reshape(parameter_field.shape)
    mixing_rows = lax.dynamic_slice_in_dim(
        mixing, lax.axis_index("mem") * members_here, members_here, 0
    )
    return (new_field, predicted, mixing_rows)


def per_device(*arrays):
    owners = lax.axis_size("mem")
    ensemble = arrays[-1].shape[0]
    swaps = owners > 1 and owners & (owners - 1) == 0 and ensemble % SUBLANES == 0
    if swaps and ensemble <= 2 * SUBLANES:
        return small_ensemble(*arrays)
    return large_ensemble(*arrays)


def solution(mesh):
    in_specs = (
        P(("grp", "mem"), "slab", None, None),
        P(("grp", "slab"), None, None),
        P(("grp", "slab")),
        P(("grp", "slab")),
        P(("grp", "slab")),
        P("grp", None),
    )
    out_specs = (
        P(("grp", "mem"), "slab", None, None),
        P(("grp", "mem"), "slab"),
        P(("grp", "mem"), None),
    )
    return jax.shard_map(
        per_device, mesh=mesh, in_specs=in_specs, out_specs=out_specs, check_vma=False
    )
```

```python
import functools

import jax
import jax.numpy as jnp
from jax import lax
from jax.experimental import pallas as pl
from jax.experimental.pallas import tpu as pltpu
from jax.sharding import PartitionSpec as P


STEPS = 3

ADVECT_SPEED = 0.1
KAPPA_BASE = 0.07
KAPPA_SWING = 0.05
STEP_SCALE = 0.02
PRIOR_VARIANCE = 0.02
EPSILON = 1e-06

LANES = 128
SUBLANES = 8

VMEM = pl.BlockSpec(memory_space=pltpu.VMEM)
SMEM = pl.BlockSpec(memory_space=pltpu.SMEM)
SMALL = pltpu.CompilerParams(vmem_limit_bytes=20 * 2**20)


def ring(axis):
    count = lax.axis_size(axis)
    forward = [(i, (i + 1) % count) for i in range(count)]
    backward = [(target, source) for source, target in forward]
    return forward, backward


def twice_flux(left, right):
    speed = jnp.maximum(jnp.abs(left), jnp.abs(right))
    return (left * left + right * right) - (speed + speed) * (right - left)


def level_shifts(center, row):
    count = center.shape[0] // SUBLANES
    tiles = [center[t * SUBLANES : (t + 1) * SUBLANES] for t in range(count)]
    down = [pltpu.roll(tile, SUBLANES - 1, 0) for tile in tiles]
    up = [pltpu.roll(tile, 1, 0) for tile in tiles]
    upper = [
        jnp.where(row == SUBLANES - 1, down[t + 1] if t + 1 < count else tiles[t], down[t])
        for t in range(count)
    ]
    lower = [jnp.where(row == 0, up[t - 1] if t else tiles[t], up[t]) for t in range(count)]
    return jnp.concatenate(upper, axis=0), jnp.concatenate(lower, axis=0)


def laplacian(below, center, above, row):
    columns = center.shape[1]
    upper, lower = level_shifts(center, row)
    return (
        above
        + below
        + upper
        + lower
        + pltpu.roll(center, 1, 1)
        + pltpu.roll(center, columns - 1, 1)
        - 6.0 * center
    )


def sweep(count, body, flux):
    if count % 2:
        return lax.fori_loop(0, count, body, flux)
    return lax.fori_loop(0, count // 2, lambda i, f: body(2 * i + 1, body(2 * i, f)), flux)


def forward_kernel(
    line_ref,
    index_ref,
    tracer_ref,
    param_ref,
    below_ref,
    above_ref,
    low_ref,
    high_ref,
    observed_ref,
    variance_ref,
    out_ref,
    seen_ref,
    target_ref,
    weight_ref,
    ext,
    kappa,
    buf_a,
    buf_b,
    table,
    stage,
):
    members, width, levels, columns = param_ref.shape
    rim = STEPS - 1
    halves = columns // LANES
    pitch = SUBLANES
    row = lax.broadcasted_iota(jnp.int32, (SUBLANES, columns), 0)

    target_ref[...] = observed_ref[...]
    weight_ref[...] = variance_ref[...]
    for i in range(STEPS):
        ext[i] = below_ref[below_ref.shape[0] - STEPS + i]
        ext[STEPS + width + i] = above_ref[i]

    @pl.loop(0, width)
    def _(i):
        ext[STEPS + i] = tracer_ref[i]
        for m in range(members):
            kappa[m, rim + i] = KAPPA_BASE + KAPPA_SWING * jnp.tanh(param_ref[m, i])

    for m in range(members):
        for i in range(rim):
            kappa[m, i] = KAPPA_BASE + KAPPA_SWING * jnp.tanh(low_ref[m, i])
            kappa[m, rim + width + i] = KAPPA_BASE + KAPPA_SWING * jnp.tanh(high_ref[m, i])

    def step_first(i, flux_low):
        center, above = ext[i + 1], ext[i + 2]
        flux_high = twice_flux(center, above)
        lap = laplacian(ext[i], center, above, row)
        base = center - (0.25 * ADVECT_SPEED) * (flux_high - flux_low)
        for m in range(members):
            buf_a[m, i] = base + kappa[m, i] * lap
        return flux_high

    sweep(width + 2 * rim, step_first, twice_flux(ext[0], ext[1]))

    for number in range(1, STEPS):
        source, target = (buf_a, buf_b) if number % 2 else (buf_b, buf_a)
        margin = STEPS - 1 - number
        last = number == STEPS - 1
        for m in range(members):

            def step_next(i, flux_low):
                center, above = source[m, i + 1], source[m, i + 2]
                flux_high = twice_flux(center, above)
                lap = laplacian(source[m, i], center, above, row)
                new = (
                    center
                    - (0.25 * ADVECT_SPEED) * (flux_high - flux_low)
                    + kappa[m, i + number] * lap
                )
                if last:
                    for h in range(halves):
                        at = i * (levels * halves * pitch) + h * pitch + m
                        table[pl.ds(at, levels, stride=halves * pitch), :] = new[
                            :, h * LANES : (h + 1) * LANES
                        ]
                else:
                    target[m, i] = new
                return flux_high

            sweep(width + 2 * margin, step_next, twice_flux(source[m, 0], source[m, 1]))

    sublane = lax.broadcasted_iota(jnp.int32, (LANES, LANES), 0)
    groups = out_ref.shape[1] // LANES

    for group in range(groups):
        first = group * LANES
        base = group % 2 * members * LANES
        for o in range(LANES):
            at = pl.multiple_of(line_ref[first + o], pitch)
            stage[base + o * members : base + (o + 1) * members, :] = table[
                pl.ds(at, members), :
            ]
        wanted = sublane == (index_ref[group : group + 1, :] & (LANES - 1))
        for m in range(members):
            turned = stage[pl.ds(base + m, LANES, stride=members), :].T
            picked = jnp.sum(jnp.where(wanted, turned, 0.0), axis=0, keepdims=True)
            out_ref[m : m + 1, first : first + LANES] = picked
            seen_ref[0, m * groups + group : m * groups + group + 1, :] = picked
    for b in range(1, seen_ref.shape[0]):
        seen_ref[b] = seen_ref[0]


def forward_observe(index, tracer, param, layers, params, observed, variance, copies=1):
    members, width, levels, columns = param.shape
    count = index.shape[0]
    rim = STEPS - 1
    rows = width * levels * (columns // LANES) * SUBLANES
    cell = index - lax.axis_index("slab") * (width * levels * columns)
    return pl.pallas_call(
        forward_kernel,
        out_shape=(
            jax.ShapeDtypeStruct((members, count), jnp.float32),
            jax.ShapeDtypeStruct((copies, members * count // LANES, LANES), jnp.float32),
            jax.ShapeDtypeStruct((count // LANES, LANES), jnp.float32),
            jax.ShapeDtypeStruct((count // LANES, LANES), jnp.float32),
        ),
        in_specs=[SMEM] + [VMEM] * 9,
        out_specs=(VMEM,) * 4,
        scratch_shapes=[
            pltpu.VMEM((width + 2 * STEPS, levels, columns), jnp.float32),
            pltpu.VMEM((members, width + 2 * rim, levels, columns), jnp.float32),
            pltpu.VMEM((members, width + 2 * rim, levels, columns), jnp.float32),
            pltpu.VMEM((members, width + 2 * rim, levels, columns), jnp.float32),
            pltpu.VMEM((rows, LANES), jnp.float32),
            pltpu.VMEM((2 * members * LANES, LANES), jnp.float32),
        ],
        cost_estimate=pl.CostEstimate(
            flops=100 * param.size, bytes_accessed=16 * param.size, transcendentals=param.size
        ),
        compiler_params=SMALL,
        name="forward_observe",
    )(
        lax.shift_right_logical(cell, 7) * SUBLANES,
        index.reshape(-1, LANES),
        tracer,
        param,
        *layers,
        *params,
        observed.reshape(-1, LANES),
        variance.reshape(-1, LANES),
    )


def gram_kernel(order, *refs):
    owners = len(order)
    blocks = refs[:owners]
    dev_ref, mean_ref, packed_ref = refs[owners:]
    members, rows, columns = blocks[0].shape
    ensemble = owners * members
    me = lax.axis_index("mem")

    @pl.loop(0, rows // SUBLANES)
    def _(r):
        at = pl.ds(pl.multiple_of(r * SUBLANES, SUBLANES), SUBLANES)
        parts = [blocks[b][m, at, :] for b in range(owners) for m in range(members)]
        total = parts[0]
        for part in parts[1:]:
            total = total + part
        mean = total * (1.0 / ensemble)
        mean_ref[at, :] = mean
        for i, b in enumerate(order):
            for m in range(members):
                dev_ref[(me ^ b) * members + m, at, :] = parts[i * members + m] - mean

    row = lax.broadcasted_iota(jnp.int32, (SUBLANES, LANES), 0)
    lane = lax.broadcasted_iota(jnp.int32, (SUBLANES, LANES), 1)

    def fold(left, right):
        product = left * right
        while product.shape[0] > SUBLANES:
            cut = product.shape[0] // 2
            product = product[:cut] + product[cut:]
        total = product[:, :LANES]
        for h in range(1, columns // LANES):
            total = total + product[:, h * LANES : (h + 1) * LANES]
        return jnp.sum(total, axis=0, keepdims=True)

    tiles = range(0, ensemble, SUBLANES)
    upper = [jnp.zeros((SUBLANES, LANES), jnp.float32) for _ in tiles]
    shifts = [jnp.zeros((SUBLANES, LANES), jnp.float32) for _ in tiles]
    means = mean_ref[...]
    for k in range(ensemble):
        left = dev_ref[k]
        shift = fold(left, means)
        shifts[k // SUBLANES] = jnp.where(row == k % SUBLANES, shift, shifts[k // SUBLANES])
        sums = [fold(left, dev_ref[j]) for j in range(k + 1)]
        for t, first in enumerate(tiles):
            stack = None
            for j in range(first, min(first + SUBLANES, k + 1)):
                stack = sums[j] if stack is None else jnp.where(row == j - first, sums[j], stack)
            if stack is not None:
                column = jnp.sum(jnp.broadcast_to(stack, row.shape), axis=1, keepdims=True)
                upper[t] = jnp.where(lane == k, column, upper[t])
    number = lax.broadcasted_iota(jnp.int32, (ensemble, LANES), 0)
    position = lax.broadcasted_iota(jnp.int32, (ensemble, LANES), 1)
    whole = jnp.where(position >= number, jnp.concatenate(upper, axis=0), 0.0)
    square = jnp.concatenate([whole, jnp.zeros((LANES - ensemble, LANES), jnp.float32)], axis=0)
    mirrored = jnp.where(position < number, square.T[:ensemble], whole)
    mirrored = mirrored + jnp.sum(jnp.concatenate(shifts, axis=0), axis=1, keepdims=True)
    packed = jnp.zeros((SUBLANES, LANES), jnp.float32)
    for t, first in enumerate(tiles):
        part = pltpu.roll(mirrored[first : first + SUBLANES], t * ensemble, 1)
        inside = (lane >= t * ensemble) & (lane < (t + 1) * ensemble)
        packed = jnp.where(inside, part, packed)
    packed_ref[...] = packed


def gram_call(blocks, order):
    owners = len(order)
    members, rows, columns = blocks[0].shape
    ensemble = owners * members
    return pl.pallas_call(
        functools.partial(gram_kernel, order),
        out_shape=(
            jax.ShapeDtypeStruct((ensemble, rows, columns), jnp.float32),
            jax.ShapeDtypeStruct((rows, columns), jnp.float32),
            jax.ShapeDtypeStruct((SUBLANES, LANES), jnp.float32),
        ),
        in_specs=[VMEM] * owners,
        out_specs=(VMEM,) * 3,
        compiler_params=SMALL,
        name="prior_products",
    )(*blocks)


def send_kernel(prior_ref, data_ref, load_ref):
    total = prior_ref[...] + data_ref[...]
    for i in range(load_ref.shape[0]):
        load_ref[i] = total


def send_call(prior, data, copies):
    return pl.pallas_call(
        send_kernel,
        out_shape=jax.ShapeDtypeStruct((copies,) + prior.shape, jnp.float32),
        in_specs=[VMEM] * 2,
        out_specs=VMEM,
        compiler_params=SMALL,
        name="send_products",
    )(prior, data)


def pack_products(part):
    count = part.shape[0]
    halves = [part[t : t + SUBLANES] for t in range(0, count, SUBLANES)]
    wide = jnp.concatenate(halves, axis=1)
    return jnp.pad(wide, ((0, 0), (LANES // 2, LANES // 2 - wide.shape[1])))


def mix_kernel(
    total_cells, order, sums_ref, noise_ref, dev_ref, mean_ref, *refs
):
    outs = refs[: len(order)]
    rows_ref, coef = refs[len(order) :]
    ensemble, rows, columns = dev_ref.shape
    members = outs[0].shape[0]
    me = lax.axis_index("mem")

    packed = sums_ref[0]
    for i in range(1, sums_ref.shape[0]):
        packed = packed + sums_ref[i]

    def unpack(first):
        parts = [
            packed[:, first + t * ensemble : first + (t + 1) * ensemble]
            for t in range(ensemble // SUBLANES)
        ]
        return jnp.concatenate(parts, axis=0)

    data_gram = unpack(LANES // 2) * (1.0 / ensemble)
    prior_gram = unpack(0) * (1.0 / (ensemble * PRIOR_VARIANCE * total_cells))
    power = jnp.sum(data_gram * data_gram, keepdims=True) / (ensemble * ensemble)
    step_size = STEP_SCALE / jnp.sqrt(power + EPSILON)
    mixing = (
        -step_size * (data_gram + prior_gram)
        + jnp.sqrt(2.0 * step_size / ensemble) * noise_ref[...]
    )
    rows_ref[...] = mixing
    weight = mixing + jnp.where(
        lax.broadcasted_iota(jnp.int32, mixing.shape, 0)
        == lax.broadcasted_iota(jnp.int32, mixing.shape, 1),
        1.0,
        0.0,
    )
    for j in range(ensemble):
        coef[j] = jnp.broadcast_to(weight[:, j : j + 1], (ensemble, LANES))

    for out, b in zip(outs, order):
        for m in range(members):
            j = (me ^ b) * members + m

            @pl.loop(0, rows // (2 * SUBLANES))
            def _(r):
                at = pl.ds(pl.multiple_of(r * 2 * SUBLANES, 2 * SUBLANES), 2 * SUBLANES)
                total = mean_ref[at, :]
                for k in range(ensemble):
                    scale = jnp.broadcast_to(coef[j, k : k + 1, :], (2 * SUBLANES, LANES))
                    scale = jnp.concatenate([scale] * (columns // LANES), axis=1)
                    total = total + scale * dev_ref[k, at, :]
                out[m, at, :] = total


def mix_call(sums, noise, dev, mean, total_cells, order):
    ensemble, rows, columns = dev.shape
    members = ensemble // lax.axis_size("mem")
    block = jax.ShapeDtypeStruct((members, rows, columns), jnp.float32)
    result = pl.pallas_call(
        functools.partial(mix_kernel, total_cells, order),
        out_shape=(block,) * len(order)
        + (jax.ShapeDtypeStruct((ensemble, ensemble), jnp.float32),),
        in_specs=[VMEM] * 4,
        out_specs=(VMEM,) * (len(order) + 1),
        scratch_shapes=[pltpu.VMEM((ensemble, ensemble, LANES), jnp.float32)],
        compiler_params=SMALL,
        name="mix_update",
    )(sums, noise, dev, mean)
    return result[:-1], result[-1]


def cut_blocks(param, owners):
    members, width, levels, columns = param.shape
    flat = param.reshape(members, width * levels, columns)
    rows = width * levels // owners
    me = lax.axis_index("mem")
    return [
        lax.dynamic_slice_in_dim(flat, (me ^ b) * rows, rows, axis=1) for b in range(owners)
    ]


def slab_rims(tracer, param):
    rim = STEPS - 1
    forward, backward = ring("slab")
    if set(forward) == set(backward):
        moved = lax.ppermute(tracer, "slab", forward)
        layers = (moved, moved)
    else:
        layers = (
            lax.ppermute(tracer[-STEPS:], "slab", forward),
            lax.ppermute(tracer[:STEPS], "slab", backward),
        )
    params = (
        lax.ppermute(param[:, -rim:], "slab", forward),
        lax.ppermute(param[:, :rim], "slab", backward),
    )
    return layers, params


def join_kernel(order, *refs):
    owners = len(order)
    blocks = refs[:owners]
    out_ref, sem = refs[owners:]
    me = lax.axis_index("mem")
    rows = blocks[0].shape[1]
    started = []
    for i, b in enumerate(order):
        at = pl.ds(pl.multiple_of((me ^ b) * rows, rows), rows)
        started.append(pltpu.make_async_copy(blocks[i], out_ref.at[:, at], sem.at[i]))
    for copy in started:
        copy.start()
    for copy in started:
        copy.wait()


def join_call(blocks, order):
    owners = len(blocks)
    members, rows, columns = blocks[0].shape
    return pl.pallas_call(
        functools.partial(join_kernel, order),
        out_shape=jax.ShapeDtypeStruct((members, owners * rows, columns), jnp.float32),
        in_specs=[VMEM] * owners,
        out_specs=pl.BlockSpec(memory_space=pl.ANY),
        scratch_shapes=[pltpu.SemaphoreType.DMA((owners,))],
        compiler_params=SMALL,
        name="join_blocks",
    )(*blocks)


def dot32(spec, a, b):
    return jnp.einsum(
        spec, a, b, precision=lax.Precision.HIGHEST, preferred_element_type=jnp.float32
    )


def far_first(owners):
    half = owners // 2
    return (1,) + tuple(range(owners - 1, half - 1, -1)) + tuple(range(half - 1, 1, -1)) + (0,)


def swap(block, b):
    count = lax.axis_size("mem")
    return lax.ppermute(block, "mem", [(i, i ^ b) for i in range(count)])


def data_products(values, observed, variance):
    spread = values - jnp.mean(values, axis=0, keepdims=True)
    weighted = (values - observed[None]) / variance[None]
    return dot32("ko,jo->kj", spread, weighted)


def broadcast_exchange(load, axes):
    return lax.all_to_all(load, axes, split_axis=0, concat_axis=0, tiled=True)


def small_ensemble(
    parameter_field, initial_tracer, observed, observation_variance, observation_index, noise
):
    members_here, slab_width, levels, columns = parameter_field.shape
    ensemble = noise.shape[0]
    owners = lax.axis_size("mem")
    total_cells = slab_width * levels * columns * lax.axis_size("slab")

    slabs = lax.axis_size("slab")
    blocks = cut_blocks(parameter_field, owners)
    order = far_first(owners)
    layers, params = slab_rims(initial_tracer, parameter_field)
    near = []
    for b in order[:-1]:
        near.append(swap(blocks[b], b))
    near.append(blocks[0])
    predicted, seen, target, spread = forward_observe(
        observation_index,
        initial_tracer,
        parameter_field,
        layers,
        params,
        observed,
        observation_variance,
        owners,
    )
    values = broadcast_exchange(seen, "mem").reshape(ensemble, -1)
    data_part = data_products(values, target.reshape(-1), spread.reshape(-1))

    dev, mean, prior_part = gram_call(near, order)
    load = send_call(prior_part, pack_products(data_part / owners), owners * slabs)
    sums = broadcast_exchange(load, ("mem", "slab"))
    sent, mixing = mix_call(sums, noise, dev, mean, total_cells, order)
    back = [swap(block, b) for b, block in zip(order[:-1], sent)] + [sent[-1]]
    new_field = join_call(back, order).reshape(parameter_field.shape)
    mixing_rows = lax.dynamic_slice_in_dim(
        mixing, lax.axis_index("mem") * members_here, members_here, 0
    )
    return (new_field, predicted, mixing_rows)


def large_ensemble(
    parameter_field, initial_tracer, observed, observation_variance, observation_index, noise
):
    members_here, slab_width, levels, columns = parameter_field.shape
    ensemble = noise.shape[0]
    owners = lax.axis_size("mem")
    cell_rows = slab_width * levels
    rows = cell_rows // owners
    total_cells = cell_rows * columns * lax.axis_size("slab")
    layers, params = slab_rims(initial_tracer, parameter_field)
    blocks = parameter_field.reshape(members_here, owners, rows, columns).transpose(1, 0, 2, 3)
    near = lax.all_to_all(blocks, "mem", split_axis=0, concat_axis=0, tiled=True)
    predicted = forward_observe(
        observation_index,
        initial_tracer,
        parameter_field,
        layers,
        params,
        observed,
        observation_variance,
    )[0]
    flat = near.reshape(ensemble, rows * columns)
    deviation = flat - jnp.mean(flat, axis=0, keepdims=True)
    prior_part = dot32("kc,jc->kj", deviation, flat)

    values = lax.all_gather(predicted, "mem", axis=0, tiled=True)
    data_part = data_products(values, observed, observation_variance)
    data_gram = lax.psum(data_part, "slab") / ensemble
    prior_gram = lax.psum(prior_part, ("mem", "slab")) / (
        ensemble * PRIOR_VARIANCE * total_cells
    )
    step_size = STEP_SCALE / jnp.sqrt(jnp.mean(data_gram * data_gram) + EPSILON)
    mixing = -step_size * (data_gram + prior_gram) + jnp.sqrt(2.0 * step_size / ensemble) * noise
    updated = flat + dot32("kj,kc->jc", mixing, deviation)
    returned = lax.all_to_all(
        updated.reshape(owners, members_here, rows, columns),
        "mem",
        split_axis=0,
        concat_axis=0,
        tiled=True,
    )
    new_field = returned.transpose(1, 0, 2, 3).reshape(parameter_field.shape)
    mixing_rows = lax.dynamic_slice_in_dim(
        mixing, lax.axis_index("mem") * members_here, members_here, 0
    )
    return (new_field, predicted, mixing_rows)


def per_device(*arrays):
    owners = lax.axis_size("mem")
    ensemble = arrays[-1].shape[0]
    if is_small(owners, ensemble):
        return small_ensemble(*arrays)
    return large_ensemble(*arrays)


def is_small(owners, ensemble):
    swaps = owners > 1 and owners & (owners - 1) == 0 and ensemble % SUBLANES == 0
    return swaps and ensemble <= 2 * SUBLANES


def solution(mesh):
    in_specs = (
        P(("grp", "mem"), "slab", None, None),
        P(("grp", "slab"), None, None),
        P(("grp", "slab")),
        P(("grp", "slab")),
        P(("grp", "slab")),
        P("grp", None),
    )
    out_specs = (
        P(("grp", "mem"), "slab", None, None),
        P(("grp", "mem"), "slab"),
        P(("grp", "mem"), None),
    )
    return jax.shard_map(
        per_device, mesh=mesh, in_specs=in_specs, out_specs=out_specs, check_vma=False
    )
```

```python
import functools

import jax
import jax.numpy as jnp
from jax import lax
from jax.experimental import pallas as pl
from jax.experimental.pallas import tpu as pltpu
from jax.sharding import PartitionSpec as P


STEPS = 3

ADVECT_SPEED = 0.1
KAPPA_BASE = 0.07
KAPPA_SWING = 0.05
STEP_SCALE = 0.02
PRIOR_VARIANCE = 0.02
EPSILON = 1e-06

LANES = 128
SUBLANES = 8

VMEM = pl.BlockSpec(memory_space=pltpu.VMEM)
SMEM = pl.BlockSpec(memory_space=pltpu.SMEM)
SMALL = pltpu.CompilerParams(vmem_limit_bytes=4 * 2**20)
LARGE = pltpu.CompilerParams(vmem_limit_bytes=12 * 2**20)


def ring(axis):
    count = lax.axis_size(axis)
    forward = [(i, (i + 1) % count) for i in range(count)]
    backward = [(target, source) for source, target in forward]
    return forward, backward


def twice_flux(left, right):
    speed = jnp.maximum(jnp.abs(left), jnp.abs(right))
    return (left * left + right * right) - (speed + speed) * (right - left)


def level_shifts(center, row):
    count = center.shape[0] // SUBLANES
    tiles = [center[t * SUBLANES : (t + 1) * SUBLANES] for t in range(count)]
    down = [pltpu.roll(tile, SUBLANES - 1, 0) for tile in tiles]
    up = [pltpu.roll(tile, 1, 0) for tile in tiles]
    upper = [
        jnp.where(row == SUBLANES - 1, down[t + 1] if t + 1 < count else tiles[t], down[t])
        for t in range(count)
    ]
    lower = [jnp.where(row == 0, up[t - 1] if t else tiles[t], up[t]) for t in range(count)]
    return jnp.concatenate(upper, axis=0), jnp.concatenate(lower, axis=0)


def laplacian(below, center, above, row):
    columns = center.shape[1]
    upper, lower = level_shifts(center, row)
    return (
        above
        + below
        + upper
        + lower
        + pltpu.roll(center, 1, 1)
        + pltpu.roll(center, columns - 1, 1)
        - 6.0 * center
    )


def sweep(count, body, flux):
    if count % 2:
        return lax.fori_loop(0, count, body, flux)
    return lax.fori_loop(0, count // 2, lambda i, f: body(2 * i + 1, body(2 * i, f)), flux)


def forward_kernel(
    line_ref,
    index_ref,
    tracer_ref,
    param_ref,
    below_ref,
    above_ref,
    low_ref,
    high_ref,
    observed_ref,
    variance_ref,
    out_ref,
    seen_ref,
    target_ref,
    weight_ref,
    ext,
    kappa,
    buf_a,
    buf_b,
    table,
    stage,
):
    members, width, levels, columns = param_ref.shape
    rim = STEPS - 1
    halves = columns // LANES
    pitch = SUBLANES
    row = lax.broadcasted_iota(jnp.int32, (SUBLANES, columns), 0)

    share = target_ref.shape[0]
    part = lax.axis_index("mem") if seen_ref.shape[0] > 1 else 0
    mine = pl.ds(part * share, share)
    target_ref[...] = observed_ref[mine, :]
    weight_ref[...] = variance_ref[mine, :]
    for i in range(STEPS):
        ext[i] = below_ref[below_ref.shape[0] - STEPS + i]
        ext[STEPS + width + i] = above_ref[i]

    @pl.loop(0, width)
    def _(i):
        ext[STEPS + i] = tracer_ref[i]
        for m in range(members):
            kappa[m, rim + i] = KAPPA_BASE + KAPPA_SWING * jnp.tanh(param_ref[m, i])

    for m in range(members):
        for i in range(rim):
            at = low_ref.shape[1] - rim + i
            kappa[m, i] = KAPPA_BASE + KAPPA_SWING * jnp.tanh(low_ref[m, at])
            kappa[m, rim + width + i] = KAPPA_BASE + KAPPA_SWING * jnp.tanh(high_ref[m, i])

    def step_first(i, flux_low):
        center, above = ext[i + 1], ext[i + 2]
        flux_high = twice_flux(center, above)
        lap = laplacian(ext[i], center, above, row)
        base = center - (0.25 * ADVECT_SPEED) * (flux_high - flux_low)
        for m in range(members):
            buf_a[m, i] = base + kappa[m, i] * lap
        return flux_high

    sweep(width + 2 * rim, step_first, twice_flux(ext[0], ext[1]))

    for number in range(1, STEPS):
        source, target = (buf_a, buf_b) if number % 2 else (buf_b, buf_a)
        margin = STEPS - 1 - number
        last = number == STEPS - 1
        for m in range(members):

            def step_next(i, flux_low):
                center, above = source[m, i + 1], source[m, i + 2]
                flux_high = twice_flux(center, above)
                lap = laplacian(source[m, i], center, above, row)
                new = (
                    center
                    - (0.25 * ADVECT_SPEED) * (flux_high - flux_low)
                    + kappa[m, i + number] * lap
                )
                if last:
                    for h in range(halves):
                        at = i * (levels * halves * pitch) + h * pitch + m
                        table[pl.ds(at, levels, stride=halves * pitch), :] = new[
                            :, h * LANES : (h + 1) * LANES
                        ]
                else:
                    target[m, i] = new
                return flux_high

            sweep(width + 2 * margin, step_next, twice_flux(source[m, 0], source[m, 1]))

    sublane = lax.broadcasted_iota(jnp.int32, (LANES, LANES), 0)
    groups = out_ref.shape[1] // LANES

    for group in range(groups):
        first = group * LANES
        base = group % 2 * members * LANES
        for o in range(LANES):
            at = pl.multiple_of(line_ref[first + o], pitch)
            stage[base + o * members : base + (o + 1) * members, :] = table[
                pl.ds(at, members), :
            ]
        wanted = sublane == (index_ref[group : group + 1, :] & (LANES - 1))
        for m in range(members):
            turned = stage[pl.ds(base + m, LANES, stride=members), :].T
            picked = jnp.sum(jnp.where(wanted, turned, 0.0), axis=0, keepdims=True)
            out_ref[m : m + 1, first : first + LANES] = picked
            at = m * share + group % share
            seen_ref[group // share, at : at + 1, :] = picked


def forward_observe(index, tracer, param, layers, params, observed, variance, shares=1):
    members, width, levels, columns = param.shape
    count = index.shape[0]
    share = count // LANES // shares
    rim = STEPS - 1
    rows = width * levels * (columns // LANES) * SUBLANES
    cell = index - lax.axis_index("slab") * (width * levels * columns)
    return pl.pallas_call(
        forward_kernel,
        out_shape=(
            jax.ShapeDtypeStruct((members, count), jnp.float32),
            jax.ShapeDtypeStruct((shares, members * share, LANES), jnp.float32),
            jax.ShapeDtypeStruct((share, LANES), jnp.float32),
            jax.ShapeDtypeStruct((share, LANES), jnp.float32),
        ),
        in_specs=[SMEM] + [VMEM] * 9,
        out_specs=(VMEM,) * 4,
        scratch_shapes=[
            pltpu.VMEM((width + 2 * STEPS, levels, columns), jnp.float32),
            pltpu.VMEM((members, width + 2 * rim, levels, columns), jnp.float32),
            pltpu.VMEM((members, width + 2 * rim, levels, columns), jnp.float32),
            pltpu.VMEM((members, width + 2 * rim, levels, columns), jnp.float32),
            pltpu.VMEM((rows, LANES), jnp.float32),
            pltpu.VMEM((2 * members * LANES, LANES), jnp.float32),
        ],
        cost_estimate=pl.CostEstimate(
            flops=100 * param.size, bytes_accessed=16 * param.size, transcendentals=param.size
        ),
        compiler_params=LARGE,
        name="forward_observe",
    )(
        lax.shift_right_logical(cell, 7) * SUBLANES,
        index.reshape(-1, LANES),
        tracer,
        param,
        *layers,
        *params,
        observed.reshape(-1, LANES),
        variance.reshape(-1, LANES),
    )


def gram_kernel(order, *refs):
    owners = len(order)
    blocks = refs[:owners]
    dev_ref, mean_ref, packed_ref = refs[owners:]
    members, rows, columns = blocks[0].shape
    ensemble = owners * members
    me = lax.axis_index("mem")

    @pl.loop(0, rows // SUBLANES)
    def _(r):
        at = pl.ds(pl.multiple_of(r * SUBLANES, SUBLANES), SUBLANES)
        parts = [blocks[b][m, at, :] for b in range(owners) for m in range(members)]
        total = parts[0]
        for part in parts[1:]:
            total = total + part
        mean = total * (1.0 / ensemble)
        mean_ref[at, :] = mean
        for i, b in enumerate(order):
            for m in range(members):
                dev_ref[(me ^ b) * members + m, at, :] = parts[i * members + m] - mean

    row = lax.broadcasted_iota(jnp.int32, (SUBLANES, LANES), 0)
    lane = lax.broadcasted_iota(jnp.int32, (SUBLANES, LANES), 1)

    def fold(left, right):
        product = left * right
        while product.shape[0] > SUBLANES:
            cut = product.shape[0] // 2
            product = product[:cut] + product[cut:]
        total = product[:, :LANES]
        for h in range(1, columns // LANES):
            total = total + product[:, h * LANES : (h + 1) * LANES]
        return jnp.sum(total, axis=0, keepdims=True)

    tiles = range(0, ensemble, SUBLANES)
    upper = [jnp.zeros((SUBLANES, LANES), jnp.float32) for _ in tiles]
    shifts = [jnp.zeros((SUBLANES, LANES), jnp.float32) for _ in tiles]
    means = mean_ref[...]
    for k in range(ensemble):
        left = dev_ref[k]
        shift = fold(left, means)
        shifts[k // SUBLANES] = jnp.where(row == k % SUBLANES, shift, shifts[k // SUBLANES])
        sums = [fold(left, dev_ref[j]) for j in range(k + 1)]
        for t, first in enumerate(tiles):
            stack = None
            for j in range(first, min(first + SUBLANES, k + 1)):
                stack = sums[j] if stack is None else jnp.where(row == j - first, sums[j], stack)
            if stack is not None:
                column = jnp.sum(jnp.broadcast_to(stack, row.shape), axis=1, keepdims=True)
                upper[t] = jnp.where(lane == k, column, upper[t])
    number = lax.broadcasted_iota(jnp.int32, (ensemble, LANES), 0)
    position = lax.broadcasted_iota(jnp.int32, (ensemble, LANES), 1)
    whole = jnp.where(position >= number, jnp.concatenate(upper, axis=0), 0.0)
    square = jnp.concatenate([whole, jnp.zeros((LANES - ensemble, LANES), jnp.float32)], axis=0)
    mirrored = jnp.where(position < number, square.T[:ensemble], whole)
    mirrored = mirrored + jnp.sum(jnp.concatenate(shifts, axis=0), axis=1, keepdims=True)
    packed = jnp.zeros((SUBLANES, LANES), jnp.float32)
    for t, first in enumerate(tiles):
        part = pltpu.roll(mirrored[first : first + SUBLANES], t * ensemble, 1)
        inside = (lane >= t * ensemble) & (lane < (t + 1) * ensemble)
        packed = jnp.where(inside, part, packed)
    packed_ref[...] = packed


def gram_call(blocks, order):
    owners = len(order)
    members, rows, columns = blocks[0].shape
    ensemble = owners * members
    return pl.pallas_call(
        functools.partial(gram_kernel, order),
        out_shape=(
            jax.ShapeDtypeStruct((ensemble, rows, columns), jnp.float32),
            jax.ShapeDtypeStruct((rows, columns), jnp.float32),
            jax.ShapeDtypeStruct((SUBLANES, LANES), jnp.float32),
        ),
        in_specs=[VMEM] * owners,
        out_specs=(VMEM,) * 3,
        compiler_params=SMALL,
        name="prior_products",
    )(*blocks)


def send_kernel(prior_ref, data_ref, load_ref):
    total = prior_ref[...] + data_ref[...]
    for i in range(load_ref.shape[0]):
        load_ref[i] = total


def send_call(prior, data, copies):
    return pl.pallas_call(
        send_kernel,
        out_shape=jax.ShapeDtypeStruct((copies,) + prior.shape, jnp.float32),
        in_specs=[VMEM] * 2,
        out_specs=VMEM,
        compiler_params=SMALL,
        name="send_products",
    )(prior, data)


def pack_products(part):
    count = part.shape[0]
    halves = [part[t : t + SUBLANES] for t in range(0, count, SUBLANES)]
    wide = jnp.concatenate(halves, axis=1)
    return jnp.pad(wide, ((0, 0), (LANES // 2, LANES // 2 - wide.shape[1])))


def update_blocks(order, coef_ref, dev_ref, mean_ref, outs):
    ensemble, rows, columns = dev_ref.shape
    me = lax.axis_index("mem")
    for out, b in zip(outs, order):
        members = out.shape[0]
        for m in range(members):
            j = (me ^ b) * members + m

            @pl.loop(0, rows // (2 * SUBLANES))
            def _(r):
                at = pl.ds(pl.multiple_of(r * 2 * SUBLANES, 2 * SUBLANES), 2 * SUBLANES)
                total = mean_ref[at, :]
                for k in range(ensemble):
                    scale = jnp.broadcast_to(coef_ref[j, k : k + 1, :], (2 * SUBLANES, LANES))
                    scale = jnp.concatenate([scale] * (columns // LANES), axis=1)
                    total = total + scale * dev_ref[k, at, :]
                out[m, at, :] = total


def mix_kernel(total_cells, order, sums_ref, noise_ref, dev_ref, mean_ref, *refs):
    outs = refs[: len(order)]
    rows_ref, coef_ref = refs[len(order) :]
    ensemble = dev_ref.shape[0]

    packed = sums_ref[0]
    for i in range(1, sums_ref.shape[0]):
        packed = packed + sums_ref[i]

    def unpack(first):
        parts = [
            packed[:, first + t * ensemble : first + (t + 1) * ensemble]
            for t in range(ensemble // SUBLANES)
        ]
        return jnp.concatenate(parts, axis=0)

    data_gram = unpack(LANES // 2) * (1.0 / ensemble)
    prior_gram = unpack(0) * (1.0 / (ensemble * PRIOR_VARIANCE * total_cells))
    power = jnp.sum(data_gram * data_gram, keepdims=True) / (ensemble * ensemble)
    step_size = STEP_SCALE / jnp.sqrt(power + EPSILON)
    mixing = (
        -step_size * (data_gram + prior_gram)
        + jnp.sqrt(2.0 * step_size / ensemble) * noise_ref[...]
    )
    rows_ref[...] = mixing
    weight = mixing + jnp.where(
        lax.broadcasted_iota(jnp.int32, mixing.shape, 0)
        == lax.broadcasted_iota(jnp.int32, mixing.shape, 1),
        1.0,
        0.0,
    )
    for j in range(ensemble):
        coef_ref[j] = jnp.broadcast_to(weight[:, j : j + 1], (ensemble, LANES))
    update_blocks(order, coef_ref, dev_ref, mean_ref, outs)


def rest_kernel(order, coef_ref, dev_ref, mean_ref, *outs):
    update_blocks(order, coef_ref, dev_ref, mean_ref, outs)


def mix_call(sums, noise, dev, mean, total_cells, order):
    ensemble, rows, columns = dev.shape
    members = ensemble // lax.axis_size("mem")
    block = jax.ShapeDtypeStruct((members, rows, columns), jnp.float32)
    result = pl.pallas_call(
        functools.partial(mix_kernel, total_cells, order),
        out_shape=(block,) * len(order)
        + (
            jax.ShapeDtypeStruct((ensemble, ensemble), jnp.float32),
            jax.ShapeDtypeStruct((ensemble, ensemble, LANES), jnp.float32),
        ),
        in_specs=[VMEM] * 4,
        out_specs=(VMEM,) * (len(order) + 2),
        compiler_params=SMALL,
        name="mix_update",
    )(sums, noise, dev, mean)
    return list(result[:-2]), result[-2], result[-1]


def rest_call(coef, dev, mean, order):
    ensemble, rows, columns = dev.shape
    members = ensemble // lax.axis_size("mem")
    block = jax.ShapeDtypeStruct((members, rows, columns), jnp.float32)
    return list(
        pl.pallas_call(
            functools.partial(rest_kernel, order),
            out_shape=(block,) * len(order),
            in_specs=[VMEM] * 3,
            out_specs=(VMEM,) * len(order),
            compiler_params=SMALL,
            name="rest_update",
        )(coef, dev, mean)
    )


def send_blocks(param, order):
    members, width, levels, columns = param.shape
    owners = len(order)
    flat = param.reshape(members, width * levels, columns)
    rows = width * levels // owners
    me = lax.axis_index("mem")
    got = []
    for b in order:
        at = (me ^ b) * rows
        block = lax.dynamic_slice(
            flat, (0, at, 0), (members, rows, columns), allow_negative_indices=False
        )
        flat, block = lax.optimization_barrier((flat, block))
        if b:
            block = swap(block, b)
        got.append(block)
    return got


def slab_rims(tracer, param):
    rim = STEPS - 1
    forward, backward = ring("slab")
    if set(forward) == set(backward):
        layers = lax.ppermute(tracer, "slab", forward)
        params = lax.ppermute(param, "slab", forward)
        return (layers, layers), (params, params)
    layers = (
        lax.ppermute(tracer[-STEPS:], "slab", forward),
        lax.ppermute(tracer[:STEPS], "slab", backward),
    )
    params = (
        lax.ppermute(param[:, -rim:], "slab", forward),
        lax.ppermute(param[:, :rim], "slab", backward),
    )
    return layers, params


def join_kernel(order, *refs):
    owners = len(order)
    blocks = refs[:owners]
    out_ref, sem = refs[owners:]
    me = lax.axis_index("mem")
    rows = blocks[0].shape[1]
    started = []
    for i, b in enumerate(order):
        at = pl.ds(pl.multiple_of((me ^ b) * rows, rows), rows)
        started.append(pltpu.make_async_copy(blocks[i], out_ref.at[:, at], sem.at[i]))
    for copy in started:
        copy.start()
    for copy in started:
        copy.wait()


def join_call(blocks, order):
    owners = len(blocks)
    members, rows, columns = blocks[0].shape
    return pl.pallas_call(
        functools.partial(join_kernel, order),
        out_shape=jax.ShapeDtypeStruct((members, owners * rows, columns), jnp.float32),
        in_specs=[VMEM] * owners,
        out_specs=pl.BlockSpec(memory_space=pl.ANY),
        scratch_shapes=[pltpu.SemaphoreType.DMA((owners,))],
        compiler_params=SMALL,
        name="join_blocks",
    )(*blocks)


def dot32(spec, a, b):
    return jnp.einsum(
        spec, a, b, precision=lax.Precision.HIGHEST, preferred_element_type=jnp.float32
    )


def far_first(owners):
    half = owners // 2
    far = [half + b for b in range(0, half, 2)] + [half + b for b in range(1, half, 2)]
    near = list(range(2, half)) + ([1] if half > 1 else [])
    return tuple(far + near) + (0,)


def swap(block, b):
    count = lax.axis_size("mem")
    return lax.ppermute(block, "mem", [(i, i ^ b) for i in range(count)])


def data_products(values, observed, variance):
    spread = values - jnp.mean(values, axis=0, keepdims=True)
    weighted = (values - observed[None]) / variance[None]
    return dot32("ko,jo->kj", spread, weighted)


def broadcast_exchange(load, axes):
    return lax.all_to_all(load, axes, split_axis=0, concat_axis=0, tiled=True)


def small_ensemble(
    parameter_field, initial_tracer, observed, observation_variance, observation_index, noise
):
    members_here, slab_width, levels, columns = parameter_field.shape
    ensemble = noise.shape[0]
    owners = lax.axis_size("mem")
    total_cells = slab_width * levels * columns * lax.axis_size("slab")

    slabs = lax.axis_size("slab")
    order = far_first(owners)
    layers, params = slab_rims(initial_tracer, parameter_field)
    near = send_blocks(parameter_field, order)
    predicted, seen, target, spread = forward_observe(
        observation_index,
        initial_tracer,
        parameter_field,
        layers,
        params,
        observed,
        observation_variance,
        owners,
    )
    values = broadcast_exchange(seen, "mem").reshape(ensemble, -1)
    data_part = data_products(values, target.reshape(-1), spread.reshape(-1))

    dev, mean, prior_part = gram_call(near, order)
    load = send_call(prior_part, pack_products(data_part), owners * slabs)
    sums = broadcast_exchange(load, ("mem", "slab"))
    far = owners // 2
    sent, mixing, coef = mix_call(sums, noise, dev, mean, total_cells, order[:far])
    sent += rest_call(coef, dev, mean, order[far:])
    back = []
    for b, block in zip(order, sent):
        back.append(swap(block, b) if b else block)
    new_field = join_call(back, order).reshape(parameter_field.shape)
    mixing_rows = lax.dynamic_slice_in_dim(
        mixing, lax.axis_index("mem") * members_here, members_here, 0
    )
    return (new_field, predicted, mixing_rows)


def large_ensemble(
    parameter_field, initial_tracer, observed, observation_variance, observation_index, noise
):
    members_here, slab_width, levels, columns = parameter_field.shape
    ensemble = noise.shape[0]
    owners = lax.axis_size("mem")
    cell_rows = slab_width * levels
    rows = cell_rows // owners
    total_cells = cell_rows * columns * lax.axis_size("slab")
    layers, params = slab_rims(initial_tracer, parameter_field)
    blocks = parameter_field.reshape(members_here, owners, rows, columns).transpose(1, 0, 2, 3)
    near = lax.all_to_all(blocks, "mem", split_axis=0, concat_axis=0, tiled=True)
    predicted = forward_observe(
        observation_index,
        initial_tracer,
        parameter_field,
        layers,
        params,
        observed,
        observation_variance,
    )[0]
    flat = near.reshape(ensemble, rows * columns)
    deviation = flat - jnp.mean(flat, axis=0, keepdims=True)
    prior_part = dot32("kc,jc->kj", deviation, flat)

    values = lax.all_gather(predicted, "mem", axis=0, tiled=True)
    data_part = data_products(values, observed, observation_variance)
    data_gram = lax.psum(data_part, "slab") / ensemble
    prior_gram = lax.psum(prior_part, ("mem", "slab")) / (
        ensemble * PRIOR_VARIANCE * total_cells
    )
    step_size = STEP_SCALE / jnp.sqrt(jnp.mean(data_gram * data_gram) + EPSILON)
    mixing = -step_size * (data_gram + prior_gram) + jnp.sqrt(2.0 * step_size / ensemble) * noise
    updated = flat + dot32("kj,kc->jc", mixing, deviation)
    returned = lax.all_to_all(
        updated.reshape(owners, members_here, rows, columns),
        "mem",
        split_axis=0,
        concat_axis=0,
        tiled=True,
    )
    new_field = returned.transpose(1, 0, 2, 3).reshape(parameter_field.shape)
    mixing_rows = lax.dynamic_slice_in_dim(
        mixing, lax.axis_index("mem") * members_here, members_here, 0
    )
    return (new_field, predicted, mixing_rows)


def per_device(*arrays):
    owners = lax.axis_size("mem")
    ensemble = arrays[-1].shape[0]
    if is_small(owners, ensemble):
        return small_ensemble(*arrays)
    return large_ensemble(*arrays)


def is_small(owners, ensemble):
    swaps = owners > 1 and owners & (owners - 1) == 0 and ensemble % SUBLANES == 0
    return swaps and ensemble <= 2 * SUBLANES


def solution(mesh):
    in_specs = (
        P(("grp", "mem"), "slab", None, None),
        P(("grp", "slab"), None, None),
        P(("grp", "slab")),
        P(("grp", "slab")),
        P(("grp", "slab")),
        P("grp", None),
    )
    out_specs = (
        P(("grp", "mem"), "slab", None, None),
        P(("grp", "mem"), "slab"),
        P(("grp", "mem"), None),
    )
    return jax.shard_map(
        per_device, mesh=mesh, in_specs=in_specs, out_specs=out_specs, check_vma=False
    )
```

```python
import functools

import jax
import jax.numpy as jnp
from jax import lax
from jax.experimental import pallas as pl
from jax.experimental.pallas import tpu as pltpu
from jax.sharding import PartitionSpec as P


STEPS = 3

ADVECT_SPEED = 0.1
KAPPA_BASE = 0.07
KAPPA_SWING = 0.05
STEP_SCALE = 0.02
PRIOR_VARIANCE = 0.02
EPSILON = 1e-06

LANES = 128
SUBLANES = 8

VMEM = pl.BlockSpec(memory_space=pltpu.VMEM)
SMEM = pl.BlockSpec(memory_space=pltpu.SMEM)
SMALL = pltpu.CompilerParams(vmem_limit_bytes=4 * 2**20)
LARGE = pltpu.CompilerParams(vmem_limit_bytes=12 * 2**20)


def ring(axis):
    count = lax.axis_size(axis)
    forward = [(i, (i + 1) % count) for i in range(count)]
    backward = [(target, source) for source, target in forward]
    return forward, backward


def twice_flux(left, right):
    speed = jnp.maximum(jnp.abs(left), jnp.abs(right))
    return (left * left + right * right) - (speed + speed) * (right - left)


def level_shifts(center, row):
    count = center.shape[0] // SUBLANES
    tiles = [center[t * SUBLANES : (t + 1) * SUBLANES] for t in range(count)]
    down = [pltpu.roll(tile, SUBLANES - 1, 0) for tile in tiles]
    up = [pltpu.roll(tile, 1, 0) for tile in tiles]
    upper = [
        jnp.where(row == SUBLANES - 1, down[t + 1] if t + 1 < count else tiles[t], down[t])
        for t in range(count)
    ]
    lower = [jnp.where(row == 0, up[t - 1] if t else tiles[t], up[t]) for t in range(count)]
    return jnp.concatenate(upper, axis=0), jnp.concatenate(lower, axis=0)


def laplacian(below, center, above, row):
    columns = center.shape[1]
    upper, lower = level_shifts(center, row)
    return (
        above
        + below
        + upper
        + lower
        + pltpu.roll(center, 1, 1)
        + pltpu.roll(center, columns - 1, 1)
        - 6.0 * center
    )


def sweep(count, body, flux):
    if count % 2:
        return lax.fori_loop(0, count, body, flux)
    return lax.fori_loop(0, count // 2, lambda i, f: body(2 * i + 1, body(2 * i, f)), flux)


def forward_kernel(
    share,
    line_ref,
    index_ref,
    tracer_ref,
    param_ref,
    low_ref,
    high_ref,
    out_ref,
    seen_ref,
    ext,
    kappa,
    buf_a,
    buf_b,
    table,
    stage,
):
    members, width, levels, columns = param_ref.shape
    rim = STEPS - 1
    halves = columns // LANES
    pitch = SUBLANES
    row = lax.broadcasted_iota(jnp.int32, (SUBLANES, columns), 0)

    for i in range(STEPS):
        ext[i] = low_ref[i]
        ext[STEPS + width + i] = high_ref[i]

    @pl.loop(0, width)
    def _(i):
        ext[STEPS + i] = tracer_ref[i]
        for m in range(members):
            kappa[m, rim + i] = KAPPA_BASE + KAPPA_SWING * jnp.tanh(param_ref[m, i])

    for m in range(members):
        for i in range(rim):
            at = STEPS + m * rim + i
            kappa[m, i] = KAPPA_BASE + KAPPA_SWING * jnp.tanh(low_ref[at])
            kappa[m, rim + width + i] = KAPPA_BASE + KAPPA_SWING * jnp.tanh(high_ref[at])

    def step_first(i, flux_low):
        center, above = ext[i + 1], ext[i + 2]
        flux_high = twice_flux(center, above)
        lap = laplacian(ext[i], center, above, row)
        base = center - (0.25 * ADVECT_SPEED) * (flux_high - flux_low)
        for m in range(members):
            buf_a[m, i] = base + kappa[m, i] * lap
        return flux_high

    sweep(width + 2 * rim, step_first, twice_flux(ext[0], ext[1]))

    for number in range(1, STEPS):
        source, target = (buf_a, buf_b) if number % 2 else (buf_b, buf_a)
        margin = STEPS - 1 - number
        last = number == STEPS - 1
        for m in range(members):

            def step_next(i, flux_low):
                center, above = source[m, i + 1], source[m, i + 2]
                flux_high = twice_flux(center, above)
                lap = laplacian(source[m, i], center, above, row)
                new = (
                    center
                    - (0.25 * ADVECT_SPEED) * (flux_high - flux_low)
                    + kappa[m, i + number] * lap
                )
                if last:
                    for h in range(halves):
                        at = i * (levels * halves * pitch) + h * pitch + m
                        table[pl.ds(at, levels, stride=halves * pitch), :] = new[
                            :, h * LANES : (h + 1) * LANES
                        ]
                else:
                    target[m, i] = new
                return flux_high

            sweep(width + 2 * margin, step_next, twice_flux(source[m, 0], source[m, 1]))

    sublane = lax.broadcasted_iota(jnp.int32, (LANES, LANES), 0)
    groups = out_ref.shape[1] // LANES

    for group in range(groups):
        first = group * LANES
        base = group % 2 * members * LANES
        for o in range(LANES):
            at = pl.multiple_of(line_ref[first + o], pitch)
            stage[base + o * members : base + (o + 1) * members, :] = table[
                pl.ds(at, members), :
            ]
        wanted = sublane == (index_ref[group : group + 1, :] & (LANES - 1))
        for m in range(members):
            turned = stage[pl.ds(base + m, LANES, stride=members), :].T
            picked = jnp.sum(jnp.where(wanted, turned, 0.0), axis=0, keepdims=True)
            out_ref[m : m + 1, first : first + LANES] = picked
            at = (group // share * members + m) * share + group % share
            seen_ref[at : at + 1, :] = picked


def forward_observe(index, tracer, param, low, high, shares=1):
    members, width, levels, columns = param.shape
    count = index.shape[0]
    share = count // LANES // shares
    rim = STEPS - 1
    rows = width * levels * (columns // LANES) * SUBLANES
    cell = index - lax.axis_index("slab") * (width * levels * columns)
    return pl.pallas_call(
        functools.partial(forward_kernel, share),
        out_shape=(
            jax.ShapeDtypeStruct((members, count), jnp.float32),
            jax.ShapeDtypeStruct((shares * members * share, LANES), jnp.float32),
        ),
        in_specs=[SMEM] + [VMEM] * 5,
        out_specs=(VMEM,) * 2,
        scratch_shapes=[
            pltpu.VMEM((width + 2 * STEPS, levels, columns), jnp.float32),
            pltpu.VMEM((members, width + 2 * rim, levels, columns), jnp.float32),
            pltpu.VMEM((members, width + 2 * rim, levels, columns), jnp.float32),
            pltpu.VMEM((members, width + 2 * rim, levels, columns), jnp.float32),
            pltpu.VMEM((rows, LANES), jnp.float32),
            pltpu.VMEM((2 * members * LANES, LANES), jnp.float32),
        ],
        cost_estimate=pl.CostEstimate(
            flops=100 * param.size, bytes_accessed=16 * param.size, transcendentals=param.size
        ),
        compiler_params=LARGE,
        name="forward_observe",
    )(
        lax.shift_right_logical(cell, 7) * SUBLANES,
        index.reshape(-1, LANES),
        tracer,
        param,
        low,
        high,
    )


def gram_kernel(order, *refs):
    owners = len(order)
    blocks = refs[:owners]
    dev_ref, mean_ref, packed_ref, relay_ref = refs[owners:]
    members, rows, columns = blocks[0].shape
    ensemble = owners * members
    shared = relay_ref.shape[1]
    me = lax.axis_index("mem")
    upper_half = me // (owners // 2)

    @pl.loop(0, rows // SUBLANES)
    def _(r):
        at = pl.ds(pl.multiple_of(r * SUBLANES, SUBLANES), SUBLANES)
        wide = pl.ds(
            pl.multiple_of(r * SUBLANES + upper_half * shared, SUBLANES), SUBLANES
        )
        parts = [
            blocks[i][m, wide if b < owners // 2 else at, :]
            for i, b in enumerate(order)
            for m in range(members)
        ]
        total = parts[0]
        for part in parts[1:]:
            total = total + part
        mean = total * (1.0 / ensemble)
        mean_ref[at, :] = mean
        for i, b in enumerate(order):
            for m in range(members):
                dev_ref[(me ^ b) * members + m, at, :] = parts[i * members + m] - mean

    row = lax.broadcasted_iota(jnp.int32, (SUBLANES, LANES), 0)
    lane = lax.broadcasted_iota(jnp.int32, (SUBLANES, LANES), 1)

    def fold(left, right):
        product = left * right
        while product.shape[0] > SUBLANES:
            cut = product.shape[0] // 2
            product = product[:cut] + product[cut:]
        total = product[:, :LANES]
        for h in range(1, columns // LANES):
            total = total + product[:, h * LANES : (h + 1) * LANES]
        return jnp.sum(total, axis=0, keepdims=True)

    tiles = range(0, ensemble, SUBLANES)
    upper = [jnp.zeros((SUBLANES, LANES), jnp.float32) for _ in tiles]
    shifts = [jnp.zeros((SUBLANES, LANES), jnp.float32) for _ in tiles]
    means = mean_ref[...]
    for k in range(ensemble):
        left = dev_ref[k]
        shift = fold(left, means)
        shifts[k // SUBLANES] = jnp.where(row == k % SUBLANES, shift, shifts[k // SUBLANES])
        sums = [fold(left, dev_ref[j]) for j in range(k + 1)]
        for t, first in enumerate(tiles):
            stack = None
            for j in range(first, min(first + SUBLANES, k + 1)):
                stack = sums[j] if stack is None else jnp.where(row == j - first, sums[j], stack)
            if stack is not None:
                column = jnp.sum(jnp.broadcast_to(stack, row.shape), axis=1, keepdims=True)
                upper[t] = jnp.where(lane == k, column, upper[t])
    number = lax.broadcasted_iota(jnp.int32, (ensemble, LANES), 0)
    position = lax.broadcasted_iota(jnp.int32, (ensemble, LANES), 1)
    whole = jnp.where(position >= number, jnp.concatenate(upper, axis=0), 0.0)
    square = jnp.concatenate([whole, jnp.zeros((LANES - ensemble, LANES), jnp.float32)], axis=0)
    mirrored = jnp.where(position < number, square.T[:ensemble], whole)
    mirrored = mirrored + jnp.sum(jnp.concatenate(shifts, axis=0), axis=1, keepdims=True)
    packed = jnp.zeros((SUBLANES, LANES), jnp.float32)
    for t, first in enumerate(tiles):
        part = pltpu.roll(mirrored[first : first + SUBLANES], t * ensemble, 1)
        inside = (lane >= t * ensemble) & (lane < (t + 1) * ensemble)
        packed = jnp.where(inside, part, packed)
    packed_ref[...] = packed

    at = pl.ds(pl.multiple_of((1 - upper_half) * (rows - shared), SUBLANES), shared)
    for k in range(ensemble // 2):
        relay_ref[k] = dev_ref[upper_half * (ensemble // 2) + k, at, :]
    relay_ref[ensemble // 2] = mean_ref[at, :]


def gram_call(blocks, order):
    owners = len(order)
    members, rows, columns = blocks[0].shape
    ensemble = owners * members
    shared = blocks[-1].shape[1] - rows
    return pl.pallas_call(
        functools.partial(gram_kernel, order),
        out_shape=(
            jax.ShapeDtypeStruct((ensemble, rows, columns), jnp.float32),
            jax.ShapeDtypeStruct((rows, columns), jnp.float32),
            jax.ShapeDtypeStruct((SUBLANES, LANES), jnp.float32),
            jax.ShapeDtypeStruct((ensemble // 2 + 1, shared, columns), jnp.float32),
        ),
        in_specs=[VMEM] * owners,
        out_specs=(VMEM,) * 4,
        compiler_params=SMALL,
        name="prior_products",
    )(*blocks)


def send_kernel(prior_ref, values_ref, observed_ref, variance_ref, load_ref):
    copies = load_ref.shape[0]
    owners = lax.axis_size("mem")
    share = observed_ref.shape[0] // owners
    ensemble = values_ref.shape[0] // share
    first = lax.axis_index("mem") * share
    total = jnp.zeros((ensemble, LANES), jnp.float32)
    for r in range(share):
        values = values_ref[pl.ds(r, ensemble, stride=share), :]
        spread = values - jnp.sum(values, axis=0, keepdims=True) * (1.0 / ensemble)
        target = observed_ref[pl.ds(first + r, 1), :]
        weighted = (values - target) / variance_ref[pl.ds(first + r, 1), :]
        wide = jnp.concatenate(
            [weighted, jnp.zeros((LANES - ensemble, LANES), jnp.float32)], axis=0
        )
        total = total + lax.dot_general(
            spread,
            wide,
            (((1,), (1,)), ((), ())),
            precision=lax.Precision.HIGHEST,
            preferred_element_type=jnp.float32,
        )
    load = prior_ref[...]
    for t in range(ensemble // SUBLANES):
        part = total[t * SUBLANES : (t + 1) * SUBLANES]
        load = load + pltpu.roll(part, LANES // 2 + t * ensemble, 1)
    for i in range(copies):
        load_ref[i] = load


def send_call(prior, values, observed, variance, copies):
    return pl.pallas_call(
        send_kernel,
        out_shape=jax.ShapeDtypeStruct((copies,) + prior.shape, jnp.float32),
        in_specs=[VMEM] * 4,
        out_specs=VMEM,
        compiler_params=SMALL,
        name="send_products",
    )(prior, values, observed.reshape(-1, LANES), variance.reshape(-1, LANES))


def update_rows(j, m, coef_ref, dev_ref, mean_ref, source, out, target, count):
    ensemble, _, columns = dev_ref.shape
    step = 2 * SUBLANES

    @pl.loop(0, count // step)
    def _(r):
        at = pl.ds(pl.multiple_of(r * step + source, SUBLANES), step)
        to = pl.ds(pl.multiple_of(r * step + target, SUBLANES), step)
        total = mean_ref[at, :]
        for k in range(ensemble):
            scale = jnp.broadcast_to(coef_ref[j, k : k + 1, :], (step, LANES))
            scale = jnp.concatenate([scale] * (columns // LANES), axis=1)
            total = total + scale * dev_ref[k, at, :]
        out[m, to, :] = total


def mix_kernel(total_cells, order, sums_ref, noise_ref, dev_ref, mean_ref, *refs):
    outs = refs[: len(order)]
    rows_ref, coef_ref = refs[len(order) :]
    ensemble = dev_ref.shape[0]

    packed = sums_ref[0]
    for i in range(1, sums_ref.shape[0]):
        packed = packed + sums_ref[i]

    def unpack(first):
        parts = [
            packed[:, first + t * ensemble : first + (t + 1) * ensemble]
            for t in range(ensemble // SUBLANES)
        ]
        return jnp.concatenate(parts, axis=0)

    data_gram = unpack(LANES // 2) * (1.0 / ensemble)
    prior_gram = unpack(0) * (1.0 / (ensemble * PRIOR_VARIANCE * total_cells))
    power = jnp.sum(data_gram * data_gram, keepdims=True) / (ensemble * ensemble)
    step_size = STEP_SCALE / jnp.sqrt(power + EPSILON)
    mixing = (
        -step_size * (data_gram + prior_gram)
        + jnp.sqrt(2.0 * step_size / ensemble) * noise_ref[...]
    )
    rows_ref[...] = mixing
    weight = mixing + jnp.where(
        lax.broadcasted_iota(jnp.int32, mixing.shape, 0)
        == lax.broadcasted_iota(jnp.int32, mixing.shape, 1),
        1.0,
        0.0,
    )
    for j in range(ensemble):
        coef_ref[j] = jnp.broadcast_to(weight[:, j : j + 1], (ensemble, LANES))
    rows = dev_ref.shape[1]
    members, keep = outs[0].shape[:2]
    me = lax.axis_index("mem")
    source = me // (lax.axis_size("mem") // 2) * (rows - keep)
    for out, b in zip(outs, order):
        for m in range(members):
            j = (me ^ b) * members + m
            update_rows(j, m, coef_ref, dev_ref, mean_ref, source, out, 0, keep)


def rest_kernel(order, coef_ref, dev_ref, mean_ref, relay_ref, *refs):
    count = len(order)
    blocks, outs = refs[:count], refs[count : 2 * count]
    mirror_dev, mirror_mean = refs[2 * count :]
    ensemble, rows, _ = dev_ref.shape
    shared = relay_ref.shape[1]
    members = outs[0].shape[0]
    local = ensemble // 2
    me = lax.axis_index("mem")
    upper_half = me // count

    first = pl.multiple_of((1 - upper_half) * rows, SUBLANES)
    mirror_mean[...] = relay_ref[local]
    for k in range(local):
        mirror_dev[(1 - upper_half) * local + k] = relay_ref[k]
    for block, b in zip(blocks, order):
        for m in range(members):
            mirror_dev[(me ^ b) * members + m] = (
                block[m, pl.ds(first, shared), :] - mirror_mean[...]
            )
    for out, b in zip(outs, order):
        for m in range(members):
            j = (me ^ b) * members + m
            update_rows(
                j, m, coef_ref, dev_ref, mean_ref, 0, out, upper_half * shared, rows
            )
            update_rows(j, m, coef_ref, mirror_dev, mirror_mean, 0, out, first, shared)


def mix_call(sums, noise, dev, mean, total_cells, order, keep):
    ensemble, _, columns = dev.shape
    members = ensemble // lax.axis_size("mem")
    block = jax.ShapeDtypeStruct((members, keep, columns), jnp.float32)
    result = pl.pallas_call(
        functools.partial(mix_kernel, total_cells, order),
        out_shape=(block,) * len(order)
        + (
            jax.ShapeDtypeStruct((ensemble, ensemble), jnp.float32),
            jax.ShapeDtypeStruct((ensemble, ensemble, LANES), jnp.float32),
        ),
        in_specs=[VMEM] * 4,
        out_specs=(VMEM,) * (len(order) + 2),
        compiler_params=SMALL,
        name="mix_update",
    )(sums, noise, dev, mean)
    return list(result[:-2]), result[-2], result[-1]


def rest_call(coef, dev, mean, relay, blocks, order):
    ensemble, _, columns = dev.shape
    shared = relay.shape[1]
    block = jax.ShapeDtypeStruct(blocks[0].shape, jnp.float32)
    return list(
        pl.pallas_call(
            functools.partial(rest_kernel, order),
            out_shape=(block,) * len(order),
            in_specs=[VMEM] * (4 + len(order)),
            out_specs=(VMEM,) * len(order),
            scratch_shapes=[
                pltpu.VMEM((ensemble, shared, columns), jnp.float32),
                pltpu.VMEM((shared, columns), jnp.float32),
            ],
            compiler_params=SMALL,
            name="rest_update",
        )(coef, dev, mean, relay, *blocks)
    )


def row_starts(device, owners, rows, shared):
    half = owners // 2
    base = device % half * (2 * rows)
    upper = device // half
    return base + upper * rows, base + upper * (rows - shared), base + upper * (rows + shared)


def send_blocks(param, order, shared):
    members, width, levels, columns = param.shape
    owners = len(order)
    flat = param.reshape(members, width * levels, columns)
    rows = width * levels // owners
    me = lax.axis_index("mem")
    got = []
    for b in order:
        own, wide, _ = row_starts(me ^ b, owners, rows, shared)
        far = b >= owners // 2
        block = lax.dynamic_slice(
            flat,
            (0, own if far else wide, 0),
            (members, rows if far else rows + shared, columns),
            allow_negative_indices=False,
        )
        if b:
            block = swap(block, b)
        got.append(block)
    return got


def slab_rims(tracer, param):
    members, _, levels, columns = param.shape
    rim = STEPS - 1
    side = (members * rim, levels, columns)
    forward, backward = ring("slab")
    to_high = jnp.concatenate([tracer[-STEPS:], param[:, -rim:].reshape(side)], axis=0)
    to_low = jnp.concatenate([tracer[:STEPS], param[:, :rim].reshape(side)], axis=0)
    return lax.ppermute(to_high, "slab", forward), lax.ppermute(to_low, "slab", backward)


def join_kernel(order, shared, *refs):
    owners = len(order)
    blocks = refs[:owners]
    out_ref, sem = refs[owners:]
    me = lax.axis_index("mem")
    rows = out_ref.shape[1] // owners
    started = []
    for i, b in enumerate(order):
        _, wide, alone = row_starts(me ^ b, owners, rows, shared)
        first = pl.multiple_of(alone if b >= owners // 2 else wide, SUBLANES)
        at = pl.ds(first, blocks[i].shape[1])
        started.append(pltpu.make_async_copy(blocks[i], out_ref.at[:, at], sem.at[i]))
    for copy in started:
        copy.start()
    for copy in started:
        copy.wait()


def join_call(blocks, order, rows, shared):
    owners = len(blocks)
    members, _, columns = blocks[0].shape
    return pl.pallas_call(
        functools.partial(join_kernel, order, shared),
        out_shape=jax.ShapeDtypeStruct((members, owners * rows, columns), jnp.float32),
        in_specs=[VMEM] * owners,
        out_specs=pl.BlockSpec(memory_space=pl.ANY),
        scratch_shapes=[pltpu.SemaphoreType.DMA((owners,))],
        compiler_params=SMALL,
        name="join_blocks",
    )(*blocks)


def dot32(spec, a, b):
    return jnp.einsum(
        spec, a, b, precision=lax.Precision.HIGHEST, preferred_element_type=jnp.float32
    )


def far_first(owners):
    half = owners // 2
    far = [half + b for b in range(0, half, 2)] + [half + b for b in range(1, half, 2)]
    near = list(range(2, half)) + ([1] if half > 1 else [])
    return tuple(far + near) + (0,)


def back_order(owners):
    order = far_first(owners)[:-1]
    far, near = order[: owners // 2], order[owners // 2 :]
    turns = [b for pair in zip(far, near) for b in pair]
    return tuple(turns) + far[len(near) :]


def swap(block, b):
    count = lax.axis_size("mem")
    return lax.ppermute(block, "mem", [(i, i ^ b) for i in range(count)])


def data_products(values, observed, variance):
    spread = values - jnp.mean(values, axis=0, keepdims=True)
    weighted = (values - observed[None]) / variance[None]
    return dot32("ko,jo->kj", spread, weighted)


def broadcast_exchange(load, axes):
    return lax.all_to_all(load, axes, split_axis=0, concat_axis=0, tiled=True)


def small_ensemble(
    parameter_field, initial_tracer, observed, observation_variance, observation_index, noise
):
    members_here, slab_width, levels, columns = parameter_field.shape
    owners = lax.axis_size("mem")
    total_cells = slab_width * levels * columns * lax.axis_size("slab")

    slabs = lax.axis_size("slab")
    order = far_first(owners)
    low, high = slab_rims(initial_tracer, parameter_field)
    rows = slab_width * levels // owners
    shared = rows // 2
    far = owners // 2
    near = send_blocks(parameter_field, order, shared)
    predicted, seen = forward_observe(
        observation_index, initial_tracer, parameter_field, low, high, owners
    )
    values = broadcast_exchange(seen, "mem")
    dev, mean, prior_part, relay = gram_call(near, order)
    relay = swap(relay, far)
    load = send_call(prior_part, values, observed, observation_variance, owners * slabs)
    sums = broadcast_exchange(load, ("mem", "slab"))
    sent, mixing, coef = mix_call(
        sums, noise, dev, mean, total_cells, order[:far], rows - shared
    )
    sent += rest_call(coef, dev, mean, relay, near[far:], order[far:])
    updated = dict(zip(order, sent))
    back = []
    for b in back_order(owners):
        back.append(swap(updated[b], b))
    new_field = join_call(
        back + [updated[0]], back_order(owners) + (0,), rows, shared
    ).reshape(parameter_field.shape)
    mixing_rows = lax.dynamic_slice_in_dim(
        mixing, lax.axis_index("mem") * members_here, members_here, 0
    )
    return (new_field, predicted, mixing_rows)


def large_ensemble(
    parameter_field, initial_tracer, observed, observation_variance, observation_index, noise
):
    members_here, slab_width, levels, columns = parameter_field.shape
    ensemble = noise.shape[0]
    owners = lax.axis_size("mem")
    cell_rows = slab_width * levels
    rows = cell_rows // owners
    total_cells = cell_rows * columns * lax.axis_size("slab")
    low, high = slab_rims(initial_tracer, parameter_field)
    blocks = parameter_field.reshape(members_here, owners, rows, columns).transpose(1, 0, 2, 3)
    near = lax.all_to_all(blocks, "mem", split_axis=0, concat_axis=0, tiled=True)
    predicted, _ = forward_observe(
        observation_index, initial_tracer, parameter_field, low, high
    )
    flat = near.reshape(ensemble, rows * columns)
    deviation = flat - jnp.mean(flat, axis=0, keepdims=True)
    prior_part = dot32("kc,jc->kj", deviation, flat)

    values = lax.all_gather(predicted, "mem", axis=0, tiled=True)
    data_part = data_products(values, observed, observation_variance)
    data_gram = lax.psum(data_part, "slab") / ensemble
    prior_gram = lax.psum(prior_part, ("mem", "slab")) / (
        ensemble * PRIOR_VARIANCE * total_cells
    )
    step_size = STEP_SCALE / jnp.sqrt(jnp.mean(data_gram * data_gram) + EPSILON)
    mixing = -step_size * (data_gram + prior_gram) + jnp.sqrt(2.0 * step_size / ensemble) * noise
    updated = flat + dot32("kj,kc->jc", mixing, deviation)
    returned = lax.all_to_all(
        updated.reshape(owners, members_here, rows, columns),
        "mem",
        split_axis=0,
        concat_axis=0,
        tiled=True,
    )
    new_field = returned.transpose(1, 0, 2, 3).reshape(parameter_field.shape)
    mixing_rows = lax.dynamic_slice_in_dim(
        mixing, lax.axis_index("mem") * members_here, members_here, 0
    )
    return (new_field, predicted, mixing_rows)


def per_device(*arrays):
    owners = lax.axis_size("mem")
    ensemble = arrays[-1].shape[0]
    rows = arrays[0].shape[1] * arrays[0].shape[2] // owners
    if is_small(owners, ensemble, arrays[-2].shape[0]) and rows % (4 * SUBLANES) == 0:
        return small_ensemble(*arrays)
    return large_ensemble(*arrays)


def is_small(owners, ensemble, count):
    swaps = owners > 1 and owners & (owners - 1) == 0 and ensemble % SUBLANES == 0
    return swaps and ensemble <= 2 * SUBLANES and count % (owners * LANES) == 0


def solution(mesh):
    in_specs = (
        P(("grp", "mem"), "slab", None, None),
        P(("grp", "slab"), None, None),
        P(("grp", "slab")),
        P(("grp", "slab")),
        P(("grp", "slab")),
        P("grp", None),
    )
    out_specs = (
        P(("grp", "mem"), "slab", None, None),
        P(("grp", "mem"), "slab"),
        P(("grp", "mem"), None),
    )
    return jax.shard_map(
        per_device, mesh=mesh, in_specs=in_specs, out_specs=out_specs, check_vma=False
    )
```

```python
import functools

import jax
import jax.numpy as jnp
from jax import lax
from jax.experimental import pallas as pl
from jax.experimental.pallas import tpu as pltpu
from jax.sharding import PartitionSpec as P


STEPS = 3

ADVECT_SPEED = 0.1
KAPPA_BASE = 0.07
KAPPA_SWING = 0.05
STEP_SCALE = 0.02
PRIOR_VARIANCE = 0.02
EPSILON = 1e-06

LANES = 128
SUBLANES = 8

VMEM = pl.BlockSpec(memory_space=pltpu.VMEM)
SMEM = pl.BlockSpec(memory_space=pltpu.SMEM)
SMALL = pltpu.CompilerParams(vmem_limit_bytes=4 * 2**20)
LARGE = pltpu.CompilerParams(vmem_limit_bytes=12 * 2**20)


def ring(axis):
    count = lax.axis_size(axis)
    forward = [(i, (i + 1) % count) for i in range(count)]
    backward = [(target, source) for source, target in forward]
    return forward, backward


def twice_flux(left, right):
    speed = jnp.maximum(jnp.abs(left), jnp.abs(right))
    return (left * left + right * right) - (speed + speed) * (right - left)


def level_shifts(center, row):
    count = center.shape[0] // SUBLANES
    tiles = [center[t * SUBLANES : (t + 1) * SUBLANES] for t in range(count)]
    down = [pltpu.roll(tile, SUBLANES - 1, 0) for tile in tiles]
    up = [pltpu.roll(tile, 1, 0) for tile in tiles]
    upper = [
        jnp.where(row == SUBLANES - 1, down[t + 1] if t + 1 < count else tiles[t], down[t])
        for t in range(count)
    ]
    lower = [jnp.where(row == 0, up[t - 1] if t else tiles[t], up[t]) for t in range(count)]
    return jnp.concatenate(upper, axis=0), jnp.concatenate(lower, axis=0)


def laplacian(below, center, above, row):
    columns = center.shape[1]
    upper, lower = level_shifts(center, row)
    return (
        above
        + below
        + upper
        + lower
        + pltpu.roll(center, 1, 1)
        + pltpu.roll(center, columns - 1, 1)
        - 6.0 * center
    )


def sweep(count, body, flux):
    if count % 2:
        return lax.fori_loop(0, count, body, flux)
    return lax.fori_loop(0, count // 2, lambda i, f: body(2 * i + 1, body(2 * i, f)), flux)


def forward_kernel(
    share,
    line_ref,
    index_ref,
    tracer_ref,
    param_ref,
    low_ref,
    high_ref,
    out_ref,
    seen_ref,
    ext,
    kappa,
    buf_a,
    buf_b,
    table,
    stage,
):
    members, width, levels, columns = param_ref.shape
    rim = STEPS - 1
    halves = columns // LANES
    pitch = SUBLANES
    row = lax.broadcasted_iota(jnp.int32, (SUBLANES, columns), 0)

    for i in range(STEPS):
        ext[i] = low_ref[i]
        ext[STEPS + width + i] = high_ref[i]

    @pl.loop(0, width)
    def _(i):
        ext[STEPS + i] = tracer_ref[i]
        for m in range(members):
            kappa[m, rim + i] = KAPPA_BASE + KAPPA_SWING * jnp.tanh(param_ref[m, i])

    for m in range(members):
        for i in range(rim):
            at = STEPS + m * rim + i
            kappa[m, i] = KAPPA_BASE + KAPPA_SWING * jnp.tanh(low_ref[at])
            kappa[m, rim + width + i] = KAPPA_BASE + KAPPA_SWING * jnp.tanh(high_ref[at])

    def step_first(i, flux_low):
        center, above = ext[i + 1], ext[i + 2]
        flux_high = twice_flux(center, above)
        lap = laplacian(ext[i], center, above, row)
        base = center - (0.25 * ADVECT_SPEED) * (flux_high - flux_low)
        for m in range(members):
            buf_a[m, i] = base + kappa[m, i] * lap
        return flux_high

    sweep(width + 2 * rim, step_first, twice_flux(ext[0], ext[1]))

    for number in range(1, STEPS):
        source, target = (buf_a, buf_b) if number % 2 else (buf_b, buf_a)
        margin = STEPS - 1 - number
        last = number == STEPS - 1
        for m in range(members):

            def step_next(i, flux_low):
                center, above = source[m, i + 1], source[m, i + 2]
                flux_high = twice_flux(center, above)
                lap = laplacian(source[m, i], center, above, row)
                new = (
                    center
                    - (0.25 * ADVECT_SPEED) * (flux_high - flux_low)
                    + kappa[m, i + number] * lap
                )
                if last:
                    for h in range(halves):
                        at = i * (levels * halves * pitch) + h * pitch + m
                        table[pl.ds(at, levels, stride=halves * pitch), :] = new[
                            :, h * LANES : (h + 1) * LANES
                        ]
                else:
                    target[m, i] = new
                return flux_high

            sweep(width + 2 * margin, step_next, twice_flux(source[m, 0], source[m, 1]))

    sublane = lax.broadcasted_iota(jnp.int32, (LANES, LANES), 0)
    groups = out_ref.shape[1] // LANES

    for group in range(groups):
        first = group * LANES
        base = group % 2 * members * LANES
        for o in range(LANES):
            at = pl.multiple_of(line_ref[first + o], pitch)
            stage[base + o * members : base + (o + 1) * members, :] = table[
                pl.ds(at, members), :
            ]
        wanted = sublane == (index_ref[group : group + 1, :] & (LANES - 1))
        for m in range(members):
            turned = stage[pl.ds(base + m, LANES, stride=members), :].T
            picked = jnp.sum(jnp.where(wanted, turned, 0.0), axis=0, keepdims=True)
            out_ref[m : m + 1, first : first + LANES] = picked
            at = (group // share * members + m) * share + group % share
            seen_ref[at : at + 1, :] = picked


def forward_observe(index, tracer, param, low, high, shares=1):
    members, width, levels, columns = param.shape
    count = index.shape[0]
    share = count // LANES // shares
    rim = STEPS - 1
    rows = width * levels * (columns // LANES) * SUBLANES
    cell = index - lax.axis_index("slab") * (width * levels * columns)
    return pl.pallas_call(
        functools.partial(forward_kernel, share),
        out_shape=(
            jax.ShapeDtypeStruct((members, count), jnp.float32),
            jax.ShapeDtypeStruct((shares * members * share, LANES), jnp.float32),
        ),
        in_specs=[SMEM] + [VMEM] * 5,
        out_specs=(VMEM,) * 2,
        scratch_shapes=[
            pltpu.VMEM((width + 2 * STEPS, levels, columns), jnp.float32),
            pltpu.VMEM((members, width + 2 * rim, levels, columns), jnp.float32),
            pltpu.VMEM((members, width + 2 * rim, levels, columns), jnp.float32),
            pltpu.VMEM((members, width + 2 * rim, levels, columns), jnp.float32),
            pltpu.VMEM((rows, LANES), jnp.float32),
            pltpu.VMEM((2 * members * LANES, LANES), jnp.float32),
        ],
        cost_estimate=pl.CostEstimate(
            flops=100 * param.size, bytes_accessed=16 * param.size, transcendentals=param.size
        ),
        compiler_params=LARGE,
        name="forward_observe",
    )(
        lax.shift_right_logical(cell, 7) * SUBLANES,
        index.reshape(-1, LANES),
        tracer,
        param,
        low,
        high,
    )


def gram_kernel(order, *refs):
    owners = len(order)
    blocks = refs[:owners]
    dev_ref, mean_ref, packed_ref = refs[owners:]
    members, rows, columns = blocks[0].shape
    ensemble = owners * members
    me = lax.axis_index("mem")

    @pl.loop(0, rows // SUBLANES)
    def _(r):
        at = pl.ds(pl.multiple_of(r * SUBLANES, SUBLANES), SUBLANES)
        parts = [blocks[b][m, at, :] for b in range(owners) for m in range(members)]
        total = parts[0]
        for part in parts[1:]:
            total = total + part
        mean = total * (1.0 / ensemble)
        mean_ref[at, :] = mean
        for i, b in enumerate(order):
            for m in range(members):
                dev_ref[(me ^ b) * members + m, at, :] = parts[i * members + m] - mean

    row = lax.broadcasted_iota(jnp.int32, (SUBLANES, LANES), 0)
    lane = lax.broadcasted_iota(jnp.int32, (SUBLANES, LANES), 1)

    def fold(left, right):
        product = left * right
        while product.shape[0] > SUBLANES:
            cut = product.shape[0] // 2
            product = product[:cut] + product[cut:]
        total = product[:, :LANES]
        for h in range(1, columns // LANES):
            total = total + product[:, h * LANES : (h + 1) * LANES]
        return jnp.sum(total, axis=0, keepdims=True)

    tiles = range(0, ensemble, SUBLANES)
    upper = [jnp.zeros((SUBLANES, LANES), jnp.float32) for _ in tiles]
    shifts = [jnp.zeros((SUBLANES, LANES), jnp.float32) for _ in tiles]
    means = mean_ref[...]
    for k in range(ensemble):
        left = dev_ref[k]
        shift = fold(left, means)
        shifts[k // SUBLANES] = jnp.where(row == k % SUBLANES, shift, shifts[k // SUBLANES])
        sums = [fold(left, dev_ref[j]) for j in range(k + 1)]
        for t, first in enumerate(tiles):
            stack = None
            for j in range(first, min(first + SUBLANES, k + 1)):
                stack = sums[j] if stack is None else jnp.where(row == j - first, sums[j], stack)
            if stack is not None:
                column = jnp.sum(jnp.broadcast_to(stack, row.shape), axis=1, keepdims=True)
                upper[t] = jnp.where(lane == k, column, upper[t])
    number = lax.broadcasted_iota(jnp.int32, (ensemble, LANES), 0)
    position = lax.broadcasted_iota(jnp.int32, (ensemble, LANES), 1)
    whole = jnp.where(position >= number, jnp.concatenate(upper, axis=0), 0.0)
    square = jnp.concatenate([whole, jnp.zeros((LANES - ensemble, LANES), jnp.float32)], axis=0)
    mirrored = jnp.where(position < number, square.T[:ensemble], whole)
    mirrored = mirrored + jnp.sum(jnp.concatenate(shifts, axis=0), axis=1, keepdims=True)
    packed = jnp.zeros((SUBLANES, LANES), jnp.float32)
    for t, first in enumerate(tiles):
        part = pltpu.roll(mirrored[first : first + SUBLANES], t * ensemble, 1)
        inside = (lane >= t * ensemble) & (lane < (t + 1) * ensemble)
        packed = jnp.where(inside, part, packed)
    packed_ref[...] = packed


def gram_call(blocks, order):
    owners = len(order)
    members, rows, columns = blocks[0].shape
    ensemble = owners * members
    return pl.pallas_call(
        functools.partial(gram_kernel, order),
        out_shape=(
            jax.ShapeDtypeStruct((ensemble, rows, columns), jnp.float32),
            jax.ShapeDtypeStruct((rows, columns), jnp.float32),
            jax.ShapeDtypeStruct((SUBLANES, LANES), jnp.float32),
        ),
        in_specs=[VMEM] * owners,
        out_specs=(VMEM,) * 3,
        compiler_params=SMALL,
        name="prior_products",
    )(*blocks)


def send_kernel(prior_ref, values_ref, observed_ref, variance_ref, load_ref):
    copies = load_ref.shape[0]
    owners = lax.axis_size("mem")
    share = observed_ref.shape[0] // owners
    ensemble = values_ref.shape[0] // share
    first = lax.axis_index("mem") * share
    total = jnp.zeros((ensemble, LANES), jnp.float32)
    for r in range(share):
        values = values_ref[pl.ds(r, ensemble, stride=share), :]
        spread = values - jnp.sum(values, axis=0, keepdims=True) * (1.0 / ensemble)
        target = observed_ref[pl.ds(first + r, 1), :]
        weighted = (values - target) / variance_ref[pl.ds(first + r, 1), :]
        wide = jnp.concatenate(
            [weighted, jnp.zeros((LANES - ensemble, LANES), jnp.float32)], axis=0
        )
        total = total + lax.dot_general(
            spread,
            wide,
            (((1,), (1,)), ((), ())),
            precision=lax.Precision.HIGHEST,
            preferred_element_type=jnp.float32,
        )
    load = prior_ref[...]
    for t in range(ensemble // SUBLANES):
        part = total[t * SUBLANES : (t + 1) * SUBLANES]
        load = load + pltpu.roll(part, LANES // 2 + t * ensemble, 1)
    for i in range(copies):
        load_ref[i] = load


def send_call(prior, values, observed, variance, copies):
    return pl.pallas_call(
        send_kernel,
        out_shape=jax.ShapeDtypeStruct((copies,) + prior.shape, jnp.float32),
        in_specs=[VMEM] * 4,
        out_specs=VMEM,
        compiler_params=SMALL,
        name="send_products",
    )(prior, values, observed.reshape(-1, LANES), variance.reshape(-1, LANES))


def update_blocks(order, coef_ref, dev_ref, mean_ref, outs):
    ensemble, rows, columns = dev_ref.shape
    me = lax.axis_index("mem")
    for out, b in zip(outs, order):
        members = out.shape[0]
        for m in range(members):
            j = (me ^ b) * members + m

            @pl.loop(0, rows // (2 * SUBLANES))
            def _(r):
                at = pl.ds(pl.multiple_of(r * 2 * SUBLANES, 2 * SUBLANES), 2 * SUBLANES)
                total = mean_ref[at, :]
                for k in range(ensemble):
                    scale = jnp.broadcast_to(coef_ref[j, k : k + 1, :], (2 * SUBLANES, LANES))
                    scale = jnp.concatenate([scale] * (columns // LANES), axis=1)
                    total = total + scale * dev_ref[k, at, :]
                out[m, at, :] = total


def mix_kernel(total_cells, order, sums_ref, noise_ref, dev_ref, mean_ref, *refs):
    outs = refs[: len(order)]
    rows_ref, coef_ref = refs[len(order) :]
    ensemble = dev_ref.shape[0]

    packed = sums_ref[0]
    for i in range(1, sums_ref.shape[0]):
        packed = packed + sums_ref[i]

    def unpack(first):
        parts = [
            packed[:, first + t * ensemble : first + (t + 1) * ensemble]
            for t in range(ensemble // SUBLANES)
        ]
        return jnp.concatenate(parts, axis=0)

    data_gram = unpack(LANES // 2) * (1.0 / ensemble)
    prior_gram = unpack(0) * (1.0 / (ensemble * PRIOR_VARIANCE * total_cells))
    power = jnp.sum(data_gram * data_gram, keepdims=True) / (ensemble * ensemble)
    step_size = STEP_SCALE / jnp.sqrt(power + EPSILON)
    mixing = (
        -step_size * (data_gram + prior_gram)
        + jnp.sqrt(2.0 * step_size / ensemble) * noise_ref[...]
    )
    rows_ref[...] = mixing
    weight = mixing + jnp.where(
        lax.broadcasted_iota(jnp.int32, mixing.shape, 0)
        == lax.broadcasted_iota(jnp.int32, mixing.shape, 1),
        1.0,
        0.0,
    )
    for j in range(ensemble):
        coef_ref[j] = jnp.broadcast_to(weight[:, j : j + 1], (ensemble, LANES))
    update_blocks(order, coef_ref, dev_ref, mean_ref, outs)


def rest_kernel(order, coef_ref, dev_ref, mean_ref, *outs):
    update_blocks(order, coef_ref, dev_ref, mean_ref, outs)


def mix_call(sums, noise, dev, mean, total_cells, order):
    ensemble, rows, columns = dev.shape
    members = ensemble // lax.axis_size("mem")
    block = jax.ShapeDtypeStruct((members, rows, columns), jnp.float32)
    result = pl.pallas_call(
        functools.partial(mix_kernel, total_cells, order),
        out_shape=(block,) * len(order)
        + (
            jax.ShapeDtypeStruct((ensemble, ensemble), jnp.float32),
            jax.ShapeDtypeStruct((ensemble, ensemble, LANES), jnp.float32),
        ),
        in_specs=[VMEM] * 4,
        out_specs=(VMEM,) * (len(order) + 2),
        compiler_params=SMALL,
        name="mix_update",
    )(sums, noise, dev, mean)
    return list(result[:-2]), result[-2], result[-1]


def rest_call(coef, dev, mean, order):
    ensemble, rows, columns = dev.shape
    members = ensemble // lax.axis_size("mem")
    block = jax.ShapeDtypeStruct((members, rows, columns), jnp.float32)
    return list(
        pl.pallas_call(
            functools.partial(rest_kernel, order),
            out_shape=(block,) * len(order),
            in_specs=[VMEM] * 3,
            out_specs=(VMEM,) * len(order),
            compiler_params=SMALL,
            name="rest_update",
        )(coef, dev, mean)
    )


def send_blocks(param, order):
    members, width, levels, columns = param.shape
    owners = len(order)
    flat = param.reshape(members, width * levels, columns)
    rows = width * levels // owners
    me = lax.axis_index("mem")
    got = []
    for b in order:
        block = lax.dynamic_slice(
            flat, (0, (me ^ b) * rows, 0), (members, rows, columns), allow_negative_indices=False
        )
        if b:
            block = swap(block, b)
        got.append(block)
    return got


def slab_rims(tracer, param):
    members, _, levels, columns = param.shape
    rim = STEPS - 1
    side = (members * rim, levels, columns)
    forward, backward = ring("slab")
    to_high = jnp.concatenate([tracer[-STEPS:], param[:, -rim:].reshape(side)], axis=0)
    to_low = jnp.concatenate([tracer[:STEPS], param[:, :rim].reshape(side)], axis=0)
    return lax.ppermute(to_high, "slab", forward), lax.ppermute(to_low, "slab", backward)


def join_kernel(order, *refs):
    owners = len(order)
    blocks = refs[:owners]
    out_ref, sem = refs[owners:]
    me = lax.axis_index("mem")
    rows = blocks[0].shape[1]
    started = []
    for i, b in enumerate(order):
        at = pl.ds(pl.multiple_of((me ^ b) * rows, rows), rows)
        started.append(pltpu.make_async_copy(blocks[i], out_ref.at[:, at], sem.at[i]))
    for copy in started:
        copy.start()
    for copy in started:
        copy.wait()


def join_call(blocks, order):
    owners = len(blocks)
    members, rows, columns = blocks[0].shape
    return pl.pallas_call(
        functools.partial(join_kernel, order),
        out_shape=jax.ShapeDtypeStruct((members, owners * rows, columns), jnp.float32),
        in_specs=[VMEM] * owners,
        out_specs=pl.BlockSpec(memory_space=pl.ANY),
        scratch_shapes=[pltpu.SemaphoreType.DMA((owners,))],
        compiler_params=SMALL,
        name="join_blocks",
    )(*blocks)


def dot32(spec, a, b):
    return jnp.einsum(
        spec, a, b, precision=lax.Precision.HIGHEST, preferred_element_type=jnp.float32
    )


def far_first(owners):
    half = owners // 2
    far = [half + b for b in range(0, half, 2)] + [half + b for b in range(1, half, 2)]
    near = list(range(2, half)) + ([1] if half > 1 else [])
    return tuple(far + near) + (0,)


def swap(block, b):
    count = lax.axis_size("mem")
    return lax.ppermute(block, "mem", [(i, i ^ b) for i in range(count)])


def data_products(values, observed, variance):
    spread = values - jnp.mean(values, axis=0, keepdims=True)
    weighted = (values - observed[None]) / variance[None]
    return dot32("ko,jo->kj", spread, weighted)


def broadcast_exchange(load, axes):
    return lax.all_to_all(load, axes, split_axis=0, concat_axis=0, tiled=True)


def small_ensemble(
    parameter_field, initial_tracer, observed, observation_variance, observation_index, noise
):
    members_here, slab_width, levels, columns = parameter_field.shape
    owners = lax.axis_size("mem")
    total_cells = slab_width * levels * columns * lax.axis_size("slab")

    slabs = lax.axis_size("slab")
    order = far_first(owners)
    low, high = slab_rims(initial_tracer, parameter_field)
    near = send_blocks(parameter_field, order)
    predicted, seen = forward_observe(
        observation_index, initial_tracer, parameter_field, low, high, owners
    )
    values = broadcast_exchange(seen, "mem")
    dev, mean, prior_part = gram_call(near, order)
    load = send_call(prior_part, values, observed, observation_variance, owners * slabs)
    sums = broadcast_exchange(load, ("mem", "slab"))
    far = owners // 2
    sent, mixing, coef = mix_call(sums, noise, dev, mean, total_cells, order[:far])
    sent += rest_call(coef, dev, mean, order[far:])
    back = []
    for b, block in zip(order, sent):
        back.append(swap(block, b) if b else block)
    new_field = join_call(back, order).reshape(parameter_field.shape)
    mixing_rows = lax.dynamic_slice_in_dim(
        mixing, lax.axis_index("mem") * members_here, members_here, 0
    )
    return (new_field, predicted, mixing_rows)


def large_ensemble(
    parameter_field, initial_tracer, observed, observation_variance, observation_index, noise
):
    members_here, slab_width, levels, columns = parameter_field.shape
    ensemble = noise.shape[0]
    owners = lax.axis_size("mem")
    cell_rows = slab_width * levels
    rows = cell_rows // owners
    total_cells = cell_rows * columns * lax.axis_size("slab")
    low, high = slab_rims(initial_tracer, parameter_field)
    blocks = parameter_field.reshape(members_here, owners, rows, columns).transpose(1, 0, 2, 3)
    near = lax.all_to_all(blocks, "mem", split_axis=0, concat_axis=0, tiled=True)
    predicted, _ = forward_observe(
        observation_index, initial_tracer, parameter_field, low, high
    )
    flat = near.reshape(ensemble, rows * columns)
    deviation = flat - jnp.mean(flat, axis=0, keepdims=True)
    prior_part = dot32("kc,jc->kj", deviation, flat)

    values = lax.all_gather(predicted, "mem", axis=0, tiled=True)
    data_part = data_products(values, observed, observation_variance)
    data_gram = lax.psum(data_part, "slab") / ensemble
    prior_gram = lax.psum(prior_part, ("mem", "slab")) / (
        ensemble * PRIOR_VARIANCE * total_cells
    )
    step_size = STEP_SCALE / jnp.sqrt(jnp.mean(data_gram * data_gram) + EPSILON)
    mixing = -step_size * (data_gram + prior_gram) + jnp.sqrt(2.0 * step_size / ensemble) * noise
    updated = flat + dot32("kj,kc->jc", mixing, deviation)
    returned = lax.all_to_all(
        updated.reshape(owners, members_here, rows, columns),
        "mem",
        split_axis=0,
        concat_axis=0,
        tiled=True,
    )
    new_field = returned.transpose(1, 0, 2, 3).reshape(parameter_field.shape)
    mixing_rows = lax.dynamic_slice_in_dim(
        mixing, lax.axis_index("mem") * members_here, members_here, 0
    )
    return (new_field, predicted, mixing_rows)


def per_device(*arrays):
    owners = lax.axis_size("mem")
    ensemble = arrays[-1].shape[0]
    if is_small(owners, ensemble, arrays[-2].shape[0]):
        return small_ensemble(*arrays)
    return large_ensemble(*arrays)


def is_small(owners, ensemble, count):
    swaps = owners > 1 and owners & (owners - 1) == 0 and ensemble % SUBLANES == 0
    return swaps and ensemble <= 2 * SUBLANES and count % (owners * LANES) == 0


def solution(mesh):
    in_specs = (
        P(("grp", "mem"), "slab", None, None),
        P(("grp", "slab"), None, None),
        P(("grp", "slab")),
        P(("grp", "slab")),
        P(("grp", "slab")),
        P("grp", None),
    )
    out_specs = (
        P(("grp", "mem"), "slab", None, None),
        P(("grp", "mem"), "slab"),
        P(("grp", "mem"), None),
    )
    return jax.shard_map(
        per_device, mesh=mesh, in_specs=in_specs, out_specs=out_specs, check_vma=False
    )
```
